512 devices in a mesh: seq: 64 (over z, y_hi, core), head: 8 (over x, y_lo).
Axes of the slice: x: 4, y: 8 (y_hi: 4, y_lo: 2; y = y_hi * 2 + y_lo), z: 8, core: 2. Of those that a mesh axis runs over, the one named last changes fastest.
Arguments:
- block_query_rows: bfloat16 [8192, 5120], P('seq', 'head'), may hold values from -180 to 180
- block_key_rows: bfloat16 [8192, 1024], P('seq', 'head'), may hold values from -6 to 6
- block_value_rows: bfloat16 [8192, 1024], P('seq', 'head'), may hold values from -6 to 6
- stretch_segments: int32 [8192], P('seq'), may hold values from 0 to 15, never falling along the last dimension, each value on 1 to 6144 neighbouring positions
- residual: bfloat16 [8192, 5120], P('seq', 'head'), may hold values from -6 to 6
- out_weight: bfloat16 [5120, 5120], P('head', 'seq'), may hold values from -0.25 to 0.25
- cache_by_prefill: bfloat16 [2, 2, 2048, 16, 1024], P(None, None, 'seq', None, 'head'), may hold values from -6 to 6
- request_pages: int32 [128], replicated, may hold values from 1 to 64, as said below
- request_owner: int32 [128], replicated, may hold values from 0 to 63, as said below
Outputs:
- layer_out: bfloat16 [8192, 5120], P('seq', 'head')
- cache_decode: bfloat16 [2, 2, 4096, 16, 1024], P(None, None, 'seq', None, 'head')
The draws below stay inside these ranges and needn't reach their ends.
Inputs may be any that keep to these rules, and one draw needn't show every extreme that they name: `stretch_segments`: each request of the block holds at most 6144 tokens, and some request exactly that many. `request_pages`: the requests of one decode device hold at most 64 pages together, and those of some device exactly 64. `request_owner`: never falls along the requests; every device owns at least one request.
All inputs are finite; a program needn't handle non-finite values.
Results may differ from the reference program's by a relative error of at most 0.0065.
Values may be sent and summed in bfloat16 or wider, within the bound.
A program may use at most 128 MiB of HBM per device.

```python
import math
import jax
import jax.numpy as jnp
import numpy as np
from jax import lax

D = 5120
QUERY_HEADS = 40
KEY_VALUE_HEADS = 8
HEAD_SIZE = 128
NSEG = 16
PAGE_TOKENS = 16
INDEX_PAGES = 32
CACHED_LAYERS = 2
BLOCK_TOKENS = 8192
CAP = 64
N_SEQ = 64


def query_key_fields(key):
    base = jax.random.fold_in(key, 29)
    query_key, random_key = jax.random.split(base)
    sampled_keys = jnp.clip(jax.random.normal(random_key, (BLOCK_TOKENS, KEY_VALUE_HEADS * HEAD_SIZE), jnp.float32), -6.0, 6.0)
    queries = jnp.clip(jax.random.normal(query_key, (BLOCK_TOKENS, QUERY_HEADS * HEAD_SIZE), jnp.float32), -6.0, 6.0)
    return (queries, sampled_keys)


def draw_block_query_rows(key, part):
    return query_key_fields(key)[0].astype(jnp.bfloat16)


def draw_block_key_rows(key, part):
    return query_key_fields(key)[1].astype(jnp.bfloat16)


def request_plan(key):
    base = jax.random.fold_in(key, 43)
    devices_seq = N_SEQ
    half = devices_seq // 2
    streams = jax.random.split(base, 5)
    split_pages = jax.random.randint(streams[0], (half,), 3, 2 * INDEX_PAGES - 2)
    loads = jnp.stack([split_pages, 2 * INDEX_PAGES - split_pages], axis=1).reshape(devices_seq)
    first_load = jax.random.randint(streams[1], (), 3, INDEX_PAGES - 1)
    second_load = jax.random.randint(streams[2], (), 3, INDEX_PAGES - 1)
    loads = loads.at[0].set(2 * INDEX_PAGES).at[1].set(first_load).at[2].set(second_load).at[3].set(2 * INDEX_PAGES - first_load - second_load)
    count_half = jax.random.randint(streams[3], (half,), 1, 4)
    counts = jnp.stack([count_half, 4 - count_half], axis=1).reshape(devices_seq)
    counts = counts.at[0].set(1).at[1].set(3)
    raw_cuts = jax.random.randint(streams[4], (devices_seq, 2), 0, 1 << 20)
    cut_two = 1 + raw_cuts[:, 0] % jnp.maximum(loads - 1, 1)
    cut_three = 1 + raw_cuts[:, 0] % jnp.maximum(loads - 2, 1)
    cut_second = 1 + raw_cuts[:, 1] % jnp.maximum(loads - 1 - cut_three, 1)
    first_len = jnp.where(counts == 1, loads, jnp.where(counts == 2, cut_two, cut_three))
    second_len = jnp.where(counts == 2, loads - cut_two, jnp.where(counts == 3, cut_second, 0))
    third_len = jnp.where(counts == 3, loads - cut_three - cut_second, 0)
    slot_pages = jnp.stack([first_len, second_len, third_len], axis=1).reshape(-1)
    active = (jnp.arange(3, dtype=jnp.int32)[None, :] < counts[:, None]).reshape(-1)
    position = jnp.cumsum(active.astype(jnp.int32)) - 1
    target = jnp.where(active, position, 2 * devices_seq)
    owner_ids = jnp.repeat(jnp.arange(devices_seq, dtype=jnp.int32), 3)
    pages = jnp.zeros((2 * devices_seq,), jnp.int32).at[target].set(slot_pages.astype(jnp.int32), mode='drop')
    owners = jnp.zeros((2 * devices_seq,), jnp.int32).at[target].set(owner_ids, mode='drop')
    return (pages, owners)


def draw_request_pages(key, part):
    return request_plan(key)[0]


def draw_request_owner(key, part):
    return request_plan(key)[1]


def strengthened(array, stream_key, source, target, blocks, factor):
    owner, partner = [(jnp.arange(array.shape[axis_at]) // (array.shape[axis_at] // blocks)).reshape([-1 if axis == axis_at else 1 for axis in range(array.ndim)]) for axis_at in (source, target)]
    chosen = jax.random.permutation(stream_key, blocks)[partner]
    strong = (owner == chosen) | (owner == (partner + blocks // 2) % blocks)
    return jnp.where(strong, factor * array, array)


def level_of(stream_key, dims, cuts, least, high):
    gain = 1.0
    for dim, parts in cuts:
        steps = jax.random.uniform(jax.random.fold_in(jax.random.fold_in(stream_key, 6), dim), (parts,), jnp.float32, least / len(cuts), high / len(cuts))
        gain = gain * jnp.repeat(jnp.exp(steps), dims[dim] // parts).reshape((-1,) + (1,) * (len(dims) - 1 - dim))
    return gain


def length_profile(amount, total, most, lean):
    portions = [(1 << 20) // math.isqrt(grade ** lean) + 1 for grade in range(2, amount + 1)]
    spare, holding = total - most - (amount - 1), [1] * (amount - 1)
    while spare > 0:
        candidates = [i for i in range(amount - 1) if holding[i] < most]
        pool, remaining = sum([portions[i] for i in candidates]), spare
        for i in candidates:
            extra = min(most - holding[i], max(1, remaining * portions[i] // pool), spare)
            holding[i] = holding[i] + extra
            spare = spare - extra
    return np.array([most] + holding)


def uneven(key, count, total, most, slope):
    if count == 2:
        one = jax.random.randint(key, (), max(1, total - most), min(most, total - 1) + 1)
        return jnp.stack([one, total - one])
    sizes = jnp.asarray(length_profile(count, total, most, slope), jnp.int32)
    couples = (count - 1) // 2
    donor, sink = sizes[1:1 + 2 * couples:2], sizes[2:2 + 2 * couples:2]
    slack = jnp.minimum(donor - 1, most - sink)
    shifted = jax.random.randint(jax.random.fold_in(key, 1), (couples,), 0, 1 << 20) % (slack + 1)
    sizes = sizes.at[1:1 + 2 * couples:2].set(donor - shifted).at[2:2 + 2 * couples:2].set(sink + shifted)
    return sizes[jax.random.permutation(jax.random.fold_in(key, 2), count)]


def noise(rng, dims, spread, most, cuts=(), held_as=jnp.bfloat16):
    loudness = level_of(rng, dims, cuts, -0.22, 0.18) if cuts else 1.0
    drawn = jax.random.normal(rng, dims, jnp.float32) * spread * loudness
    return jnp.minimum(jnp.maximum(drawn, -most), most).astype(held_as)


def bell_draw_with(own_key, dims, spread, limit, shards, heavy, kind=jnp.bfloat16):
    values = spread * jax.random.normal(own_key, dims, jnp.float32)
    if shards:
        values = values * level_of(own_key, dims, shards, -0.22, 0.18)
    return jnp.clip(strengthened(values, jax.random.fold_in(own_key, 3), *heavy), -limit, limit).astype(kind)


def setup_inputs(seed: int = 0) -> dict:
    arg_keys = jax.random.split(jax.random.key(seed), 10)
    return {
        "block_query_rows": draw_block_query_rows(jax.random.fold_in(arg_keys[9], 71), 0),
        "block_key_rows": draw_block_key_rows(jax.random.fold_in(arg_keys[9], 71), 0),
        "block_value_rows": noise(arg_keys[2], (BLOCK_TOKENS, KEY_VALUE_HEADS * HEAD_SIZE), 1.0, 6.0, ((0, 64), (1, 8))),
        "stretch_segments": jnp.searchsorted(jnp.cumsum(uneven(arg_keys[3], NSEG, BLOCK_TOKENS, 3 * BLOCK_TOKENS // 4, 2)), jnp.arange(BLOCK_TOKENS), side="right").astype(jnp.int32),
        "residual": noise(arg_keys[4], (BLOCK_TOKENS, D), 1.0, 6.0, ((0, 64), (1, 8))),
        "out_weight": bell_draw_with(arg_keys[5], (QUERY_HEADS * HEAD_SIZE, D), (QUERY_HEADS * HEAD_SIZE) ** -0.5, 0.25, ((0, 8), (1, 64)), (0, 1, 64, 4.0)),
        "cache_by_prefill": noise(arg_keys[6], (CACHED_LAYERS, 2, INDEX_PAGES * N_SEQ, PAGE_TOKENS, KEY_VALUE_HEADS * HEAD_SIZE), 1.0, 6.0, ((2, 64), (4, 8))),
        "request_pages": draw_request_pages(jax.random.fold_in(arg_keys[9], 71), 0),
        "request_owner": draw_request_owner(jax.random.fold_in(arg_keys[9], 71), 0),
    }


def reference(block_query_rows, block_key_rows, block_value_rows, stretch_segments, residual, out_weight, cache_by_prefill, request_pages, request_owner):
    query_groups = QUERY_HEADS // KEY_VALUE_HEADS
    prefill_block = math.gcd(BLOCK_TOKENS, 256)
    widened_keys = block_key_rows.astype(jnp.float32).reshape(BLOCK_TOKENS, KEY_VALUE_HEADS, HEAD_SIZE)
    widened_values = block_value_rows.astype(jnp.float32).reshape(BLOCK_TOKENS, KEY_VALUE_HEADS, HEAD_SIZE)
    positions = jnp.arange(BLOCK_TOKENS, dtype=jnp.int32)

    def one_block(index):
        block_start = (index * prefill_block).astype(jnp.int32)
        block_queries = lax.dynamic_slice_in_dim(block_query_rows, block_start, prefill_block, 0).astype(jnp.float32).reshape(prefill_block, KEY_VALUE_HEADS, query_groups, HEAD_SIZE)
        segment_block = lax.dynamic_slice_in_dim(stretch_segments, block_start, prefill_block, 0)
        position_block = block_start + jnp.arange(prefill_block, dtype=jnp.int32)
        scores = jnp.einsum("tkgd,pkd->kgtp", block_queries, widened_keys) * (HEAD_SIZE ** -0.5)
        allowed = (segment_block[:, None] == stretch_segments[None, :]) & (position_block[:, None] >= positions[None, :])
        masked = jnp.where(allowed, scores, -1e30)
        highest = jnp.max(masked, axis=-1, keepdims=True)
        weights = jnp.where(allowed, jnp.exp(masked - highest), 0.0)
        rounded = lax.optimization_barrier(weights.astype(jnp.bfloat16)).astype(jnp.float32)
        numerator = jnp.einsum("kgtp,pkd->tkgd", rounded, widened_values)
        total = jnp.transpose(jnp.sum(weights, axis=-1), (2, 0, 1))
        result = numerator / total[..., None]
        return result.astype(jnp.bfloat16).reshape(prefill_block, QUERY_HEADS * HEAD_SIZE)

    attention = lax.map(one_block, jnp.arange(BLOCK_TOKENS // prefill_block, dtype=jnp.int32)).reshape(BLOCK_TOKENS, QUERY_HEADS * HEAD_SIZE)
    projected = jnp.dot(attention, out_weight, preferred_element_type=jnp.float32)
    layer_out = (residual.astype(jnp.float32) + projected).astype(jnp.bfloat16)

    owners = jnp.arange(N_SEQ, dtype=jnp.int32)
    run_pages = jnp.sum(jnp.where(request_owner[None, :] == owners[:, None], request_pages[None, :], 0), axis=1)
    run_start = jnp.sum(jnp.where(request_owner[None, :] < owners[:, None], request_pages[None, :], 0), axis=1)
    slots = jnp.arange(CAP, dtype=jnp.int32)
    global_page = run_start[:, None] + slots[None, :]
    valid = slots[None, :] < run_pages[:, None]
    source_row = (global_page % N_SEQ) * INDEX_PAGES + global_page // N_SEQ
    source_row = jnp.where(valid, source_row, 0).reshape(-1).astype(jnp.int32)
    moved = jnp.take(cache_by_prefill, source_row, axis=2)
    keep = valid.reshape(-1)[None, None, :, None, None]
    cache_decode = jnp.where(keep, moved, jnp.zeros_like(moved)).astype(jnp.bfloat16)
    return layer_out, cache_decode
```

```python
import functools

import jax
import jax.numpy as jnp
from jax import lax
from jax.experimental import pallas as pl
from jax.experimental.pallas import tpu as pltpu
from jax.sharding import PartitionSpec as P

HEAD_SIZE = 128
Z = 8
Y = 4
REQUESTS = 16
MESH = pl.DeviceIdType.MESH
KEY_BLOCKS = 8


def seq_id(z, y, c):
    return z * 8 + y * 2 + c


def meet(partners):
    barrier = pltpu.get_barrier_semaphore()
    for seq in partners:
        pl.semaphore_signal(barrier, inc=1, device_id={"seq": seq}, device_id_type=MESH)
    pl.semaphore_wait(barrier, len(partners))


def gather_kernel(kv_ref, w_ref, kv_all, w_all, send_sem, recv_sem, local_sem):
    me = lax.axis_index("seq")
    z, y, c = me // 8, (me // 2) % 4, me % 2
    rows = kv_ref.shape[0]
    cut = 144
    across = seq_id(z, y, 1 - c)
    up, down = seq_id((z + 1) % Z, y, c), seq_id((z + 7) % Z, y, c)
    meet([across, up, down] + [seq_id(z, (y + a) % Y, c) for a in (1, 2, 3)])

    used = [0]
    pending = []

    def send(src, dst, device):
        i = used[0]
        used[0] += 1
        copy = pltpu.make_async_remote_copy(
            src_ref=src,
            dst_ref=dst,
            send_sem=send_sem.at[i],
            recv_sem=recv_sem.at[i],
            device_id={"seq": device},
            device_id_type=MESH,
        )
        copy.start()
        pending.append(copy)
        return copy

    def kv_at(seq, part):
        lo, hi = part
        return kv_all.at[seq, pl.ds(lo, hi - lo)]

    whole = (0, rows)
    to_core = []
    own_kv = kv_all.at[me]
    ring = {}
    ring[0, 1, 1] = send(kv_ref, own_kv, up)
    ring[0, -1, 1] = send(kv_ref, own_kv, down)
    near = {}
    for a in (1, 3, 2):
        near[a] = send(kv_ref, own_kv, seq_id(z, (y + 4 - a) % Y, c))
    to_core.append(send(kv_ref, own_kv, across))
    near_w = {}
    w_slot = y * 2 + c
    for a in (1, 3, 2):
        near_w[a] = send(w_ref, w_all.at[w_slot], seq_id(z, (y + 4 - a) % Y, c))
    to_core.append(send(w_ref, w_all.at[w_slot], across))
    local = [
        pltpu.make_async_copy(kv_ref, own_kv, local_sem.at[0]),
        pltpu.make_async_copy(w_ref, w_all.at[w_slot], local_sem.at[1]),
    ]
    for copy in local:
        copy.start()

    def start_chain(a):
        seq = seq_id(z, (y + a) % Y, c)
        near[a].wait_recv()
        block = kv_at(seq, whole)
        ring[a, 1, 1] = send(block, block, up)
        ring[a, -1, 1] = send(block, block, down)
        to_core.append(send(block, block, across))

    def advance(a, k):
        for direction, target in ((1, up), (-1, down)):
            seq = seq_id((z + 8 - direction * k) % Z, (y + a) % Y, c)
            ring[a, direction, k].wait_recv()
            part = whole
            if k == 4:
                part = (0, cut) if direction == 1 else (cut, rows)
            block = kv_at(seq, part)
            if k < 4:
                onward = block
                if k == 3:
                    onward = kv_at(seq, (0, cut) if direction == 1 else (cut, rows))
                ring[a, direction, k + 1] = send(onward, onward, target)
            to_core.append(send(block, block, across))

    order = (0, 1, 3, 2)
    for tick in range(1, 9):
        for at, a in enumerate(order):
            k = tick - at
            if k == 0:
                start_chain(a)
            elif 1 <= k <= 4:
                advance(a, k)
    for a in (1, 3, 2):
        slot = (y + a) % Y * 2 + c
        near_w[a].wait_recv()
        to_core.append(send(w_all.at[slot], w_all.at[slot], across))
    for copy in to_core:
        copy.wait_recv()
    for copy in pending:
        copy.wait_send()
    for copy in local:
        copy.wait()


def gather_blocks(kv_block, w_block, seq_count):
    sems = 84
    return pl.pallas_call(
        gather_kernel,
        name="gather_blocks",
        out_shape=(
            jax.ShapeDtypeStruct((seq_count,) + kv_block.shape, kv_block.dtype),
            jax.ShapeDtypeStruct((2 * Y,) + w_block.shape, w_block.dtype),
        ),
        in_specs=[pl.BlockSpec(memory_space=pltpu.VMEM)] * 2,
        out_specs=[pl.BlockSpec(memory_space=pl.ANY)] * 2,
        scratch_shapes=[
            pltpu.SemaphoreType.DMA((sems,)),
            pltpu.SemaphoreType.DMA((sems,)),
            pltpu.SemaphoreType.DMA((2,)),
        ],
        compiler_params=pltpu.CompilerParams(collective_id=0, has_side_effects=True),
    )(kv_block, w_block)


def ring_kernel(x_ref, all_ref, send_sem, recv_sem, local_sem):
    me = lax.axis_index("seq")
    z, y, c = me // 8, (me // 2) % 4, me % 2
    rows = x_ref.shape[0]
    half = rows // 2
    up, down = seq_id((z + 1) % Z, y, c), seq_id((z + 7) % Z, y, c)
    meet([up, down])
    pending = []
    ring = {}

    def send(src, dst, device, direction, k):
        i = 2 * (k - 1) + (direction > 0)
        copy = pltpu.make_async_remote_copy(
            src_ref=src,
            dst_ref=dst,
            send_sem=send_sem.at[i],
            recv_sem=recv_sem.at[i],
            device_id={"seq": device},
            device_id_type=MESH,
        )
        copy.start()
        pending.append(copy)
        ring[direction, k] = copy

    send(x_ref, all_ref.at[z], up, 1, 1)
    send(x_ref, all_ref.at[z], down, -1, 1)
    local = pltpu.make_async_copy(x_ref, all_ref.at[z], local_sem)
    local.start()
    for k in (1, 2, 3, 4):
        for direction, target in ((1, up), (-1, down)):
            ring[direction, k].wait_recv()
            if k < 4:
                block = all_ref.at[(z + 8 - direction * k) % Z]
                if k == 3:
                    block = block.at[pl.ds(0, half)] if direction == 1 else block.at[pl.ds(half, half)]
                send(block, block, target, direction, k + 1)
    for copy in pending:
        copy.wait_send()
    local.wait()


def ring_gather(x):
    return pl.pallas_call(
        ring_kernel,
        name="ring_gather",
        out_shape=jax.ShapeDtypeStruct((Z,) + x.shape, x.dtype),
        in_specs=[pl.BlockSpec(memory_space=pltpu.VMEM)],
        out_specs=pl.BlockSpec(memory_space=pl.ANY),
        scratch_shapes=[
            pltpu.SemaphoreType.DMA((8,)),
            pltpu.SemaphoreType.DMA((8,)),
            pltpu.SemaphoreType.DMA,
        ],
        compiler_params=pltpu.CompilerParams(collective_id=1, has_side_effects=True),
    )(x)


def attention_kernel(q_ref, seg_ref, kv_ref, out_ref, qt_ref, top_ref, sum_ref, acc_ref):
    seq_place = lax.axis_index("seq")
    tokens = q_ref.shape[0]
    groups = q_ref.shape[1] // HEAD_SIZE
    span = KEY_BLOCKS * tokens
    factor = HEAD_SIZE ** (-0.5) * 1.4426950408889634
    table = jnp.sum(kv_ref[:, 2 * tokens :, :].astype(jnp.float32), axis=0)
    ids = lax.broadcasted_iota(jnp.int32, table.shape, 0)
    first = jnp.sum(jnp.where(ids == seg_ref[...], table, 0.0), axis=0, keepdims=True)
    lowest = jnp.min(first).astype(jnp.int32)
    highest = jnp.max(first).astype(jnp.int32)
    start = jnp.concatenate([first.astype(jnp.int32)] * groups, axis=1)
    place = lax.broadcasted_iota(jnp.int32, (1, tokens), 1) + seq_place * tokens
    place = jnp.concatenate([place] * groups, axis=1)
    for g in range(groups):
        qt_ref[g * tokens : (g + 1) * tokens, :] = q_ref[:, g * HEAD_SIZE : (g + 1) * HEAD_SIZE]
    top_ref[...] = jnp.full(top_ref.shape, -1e29, jnp.float32)
    sum_ref[...] = jnp.zeros(sum_ref.shape, jnp.float32)
    acc_ref[...] = jnp.zeros(acc_ref.shape, jnp.float32)

    def step(masked, i, carry):
        blocks = pl.ds(i * KEY_BLOCKS, KEY_BLOCKS)
        keys = kv_ref[blocks, 0:tokens, :].reshape(span, HEAD_SIZE)
        values = kv_ref[blocks, tokens : 2 * tokens, :].reshape(span, HEAD_SIZE)
        scores = lax.dot_general(
            keys, qt_ref[...], (((1,), (1,)), ((), ())), preferred_element_type=jnp.float32
        )
        if masked:
            key_place = lax.broadcasted_iota(jnp.int32, scores.shape, 0) + i * span
            allowed = (key_place >= start) & (key_place <= place)
            scores = jnp.where(allowed, scores, -1e30)
        old = top_ref[...]
        top = jnp.maximum(old, jnp.max(scores, axis=0, keepdims=True))
        weights = jnp.exp2((scores - top) * factor)
        shrink = jnp.exp2((old - top) * factor)
        top_ref[...] = top
        sum_ref[...] = sum_ref[...] * shrink + jnp.sum(weights, axis=0, keepdims=True)
        acc_ref[...] = acc_ref[...] * shrink + lax.dot_general(
            values,
            weights.astype(jnp.bfloat16),
            (((0,), (0,)), ((), ())),
            preferred_element_type=jnp.float32,
        )
        return carry

    begin = lowest // span
    end = (seq_place * tokens + tokens - 1) // span + 1
    clear_begin = jnp.minimum((highest + span - 1) // span, end)
    clear_end = jnp.maximum((seq_place * tokens + 1) // span, clear_begin)
    lax.fori_loop(begin, clear_begin, functools.partial(step, True), 0)
    lax.fori_loop(clear_begin, clear_end, functools.partial(step, False), 0)
    lax.fori_loop(clear_end, end, functools.partial(step, True), 0)
    result = acc_ref[...] / sum_ref[...]
    for g in range(groups):
        columns = slice(g * tokens, (g + 1) * tokens)
        out_ref[:, g * HEAD_SIZE : (g + 1) * HEAD_SIZE] = result[:, columns].T.astype(out_ref.dtype)


def attend(queries, segments, kv_all):
    tokens, width = queries.shape
    count = tokens * (width // HEAD_SIZE)
    return pl.pallas_call(
        attention_kernel,
        name="attend",
        out_shape=jax.ShapeDtypeStruct(queries.shape, queries.dtype),
        in_specs=[pl.BlockSpec(memory_space=pltpu.VMEM)] * 3,
        out_specs=pl.BlockSpec(memory_space=pltpu.VMEM),
        scratch_shapes=[
            pltpu.VMEM((count, HEAD_SIZE), jnp.bfloat16),
            pltpu.VMEM((1, count), jnp.float32),
            pltpu.VMEM((1, count), jnp.float32),
            pltpu.VMEM((HEAD_SIZE, count), jnp.float32),
        ],
    )(queries, segments, kv_all)


def on_device(
    block_query_rows,
    block_key_rows,
    block_value_rows,
    stretch_segments,
    residual,
    out_weight,
    cache_by_prefill,
    request_pages,
    request_owner,
):
    seq_count = lax.axis_size("seq")
    head_count = lax.axis_size("head")
    seq_place = lax.axis_index("seq")
    ids = jnp.arange(REQUESTS, dtype=jnp.int32)
    before = jnp.sum((stretch_segments[None, :] < ids[:, None]).astype(jnp.float32), axis=1)
    table = jnp.broadcast_to(before[:, None], (REQUESTS, HEAD_SIZE)).astype(jnp.bfloat16)
    kv_block = jnp.concatenate([block_key_rows, block_value_rows, table], axis=0)
    kv_all, w_all = gather_blocks(kv_block, out_weight.T, seq_count)
    attention = attend(block_query_rows, stretch_segments[None, :], kv_all)
    attention_all = ring_gather(attention)
    rows, width = attention.shape
    partial_sums = lax.dot_general(
        attention_all.reshape(Z * rows, width),
        w_all.reshape(width, width),
        (((1,), (1,)), ((), ())),
        preferred_element_type=jnp.float32,
    ).astype(jnp.bfloat16)
    parts = lax.all_to_all(
        partial_sums.reshape(Z, rows, width), "head", split_axis=0, concat_axis=0, tiled=True
    )
    total = jnp.sum(parts.astype(jnp.float32), axis=0).astype(jnp.bfloat16)
    pairs = [
        ((z * 8 + rest) * head_count + h, (h * 8 + rest) * head_count + z)
        for z in range(Z)
        for rest in range(8)
        for h in range(head_count)
    ]
    mine = lax.ppermute(total, ("seq", "head"), pairs)
    layer_out = (residual.astype(jnp.float32) + mine.astype(jnp.float32)).astype(jnp.bfloat16)
    local_pages = cache_by_prefill.shape[2]
    capacity = 2 * local_pages
    per_pair = capacity // seq_count
    owners = jnp.arange(seq_count, dtype=jnp.int32)
    run_pages = jnp.sum(
        jnp.where(request_owner[None, :] == owners[:, None], request_pages[None, :], 0), axis=1
    )
    run_start = jnp.sum(
        jnp.where(request_owner[None, :] < owners[:, None], request_pages[None, :], 0), axis=1
    )
    pair_slots = jnp.arange(per_pair, dtype=jnp.int32)
    offset = (seq_place - run_start) % seq_count
    slot_index = pair_slots[None, :] * seq_count + offset[:, None]
    sending = slot_index < run_pages[:, None]
    local_index = pair_slots[None, :] + ((run_start + offset - seq_place) // seq_count)[:, None]
    local_index = jnp.where(sending, local_index, 0).reshape(-1)
    picked = jnp.take(cache_by_prefill, local_index, axis=2)
    outgoing = jnp.where(
        sending.reshape(-1)[None, None, :, None, None], picked, jnp.zeros_like(picked)
    )
    incoming = lax.all_to_all(outgoing, "seq", split_axis=2, concat_axis=2, tiled=True)
    layers, pair_kv, _, page_len, width = incoming.shape
    arranged = jnp.swapaxes(
        incoming.reshape(layers, pair_kv, seq_count, per_pair, page_len, width), 2, 3
    )
    my_start = run_start[seq_place]
    my_pages = run_pages[seq_place]
    rotated = jnp.roll(arranged, -my_start, axis=3).reshape(
        layers, pair_kv, capacity, page_len, width
    )
    keep = jnp.arange(capacity, dtype=jnp.int32) < my_pages
    cache_decode = jnp.where(keep[None, None, :, None, None], rotated, jnp.zeros_like(rotated))
    return (layer_out, cache_decode)


def solution(mesh):
    return jax.shard_map(
        on_device,
        mesh=mesh,
        in_specs=(
            P("seq", "head"),
            P("seq", "head"),
            P("seq", "head"),
            P("seq"),
            P("seq", "head"),
            P("head", "seq"),
            P(None, None, "seq", None, "head"),
            P(),
            P(),
        ),
        out_specs=(P("seq", "head"), P(None, None, "seq", None, "head")),
        check_vma=False,
    )
```

```python
import functools

import jax
import jax.numpy as jnp
from jax import lax
from jax.experimental import pallas as pl
from jax.experimental.pallas import tpu as pltpu
from jax.sharding import PartitionSpec as P

HEAD_SIZE = 128
Z = 8
Y = 4
REQUESTS = 16
MESH = pl.DeviceIdType.MESH
KEY_BLOCKS = 8


def seq_id(z, y, c):
    return z * 8 + y * 2 + c


def meet(partners):
    barrier = pltpu.get_barrier_semaphore()
    for seq in partners:
        pl.semaphore_signal(barrier, inc=1, device_id={"seq": seq}, device_id_type=MESH)
    pl.semaphore_wait(barrier, len(partners))


def gather_kernel(
    kv_ref, w_ref, page_ref, kv_all, w_all, page_out, by_z, by_y, send_sem, recv_sem, local_sem
):
    me = lax.axis_index("seq")
    z, y, c = me // 8, (me // 2) % 4, me % 2
    rows = kv_ref.shape[0]
    cut = 144
    across = seq_id(z, y, 1 - c)
    up, down = seq_id((z + 1) % Z, y, c), seq_id((z + 7) % Z, y, c)
    meet(
        [across]
        + [seq_id((z + d) % Z, y, c) for d in range(1, Z)]
        + [seq_id(z, (y + a) % Y, c) for a in (1, 2, 3)]
    )

    used = [0]
    pending = []

    def send(src, dst, device):
        i = used[0]
        used[0] += 1
        copy = pltpu.make_async_remote_copy(
            src_ref=src,
            dst_ref=dst,
            send_sem=send_sem.at[i],
            recv_sem=recv_sem.at[i],
            device_id={"seq": device},
            device_id_type=MESH,
        )
        copy.start()
        pending.append(copy)
        return copy

    def kv_at(seq, part):
        lo, hi = part
        return kv_all.at[seq, pl.ds(lo, hi - lo)]

    whole = (0, rows)
    to_core = []
    own_kv = kv_all.at[me]
    ring = {}
    ring[0, 1, 1] = send(kv_ref, own_kv, up)
    ring[0, -1, 1] = send(kv_ref, own_kv, down)
    near = {}
    for a in (1, 3, 2):
        near[a] = send(kv_ref, own_kv, seq_id(z, (y + 4 - a) % Y, c))
    to_core.append(send(kv_ref, own_kv, across))
    w_slot = y * 2 + c
    local = [
        pltpu.make_async_copy(kv_ref, own_kv, local_sem.at[0]),
        pltpu.make_async_copy(w_ref, w_all.at[w_slot], local_sem.at[1]),
        pltpu.make_async_copy(page_ref.at[z, y], by_z.at[z, y], local_sem.at[2]),
    ]
    for copy in local:
        copy.start()

    def start_chain(a):
        seq = seq_id(z, (y + a) % Y, c)
        near[a].wait_recv()
        block = kv_at(seq, whole)
        ring[a, 1, 1] = send(block, block, up)
        ring[a, -1, 1] = send(block, block, down)
        to_core.append(send(block, block, across))

    def advance(a, k):
        for direction, target in ((1, up), (-1, down)):
            seq = seq_id((z + 8 - direction * k) % Z, (y + a) % Y, c)
            ring[a, direction, k].wait_recv()
            part = whole
            if k == 4:
                part = (0, cut) if direction == 1 else (cut, rows)
            block = kv_at(seq, part)
            if k < 4:
                onward = block
                if k == 3:
                    onward = kv_at(seq, (0, cut) if direction == 1 else (cut, rows))
                ring[a, direction, k + 1] = send(onward, onward, target)
            to_core.append(send(block, block, across))

    page_z = {}
    page_y = {}

    def pages_over_z(d):
        to = (z + d) % Z
        page_z[d] = send(page_ref.at[to], by_z.at[z], seq_id(to, y, c))

    def pages_over_y(d):
        if d:
            page_z[d].wait_recv()
        source = (z + 8 - d) % Z
        held = by_z if d else page_ref
        for a in (1, 3, 2):
            to = (y + a) % Y
            page_y[d, a] = send(held.at[source, to], by_y.at[source, y], seq_id(z, to, c))

    near_w = {}

    def send_weight():
        for a in (1, 3, 2):
            near_w[a] = send(w_ref, w_all.at[w_slot], seq_id(z, (y + 4 - a) % Y, c))
        to_core.append(send(w_ref, w_all.at[w_slot], across))

    extra = {
        1: [(pages_over_z, 4), (pages_over_y, 0)],
        2: [(pages_over_z, 3), (pages_over_z, 5)],
        3: [(pages_over_z, 2), (pages_over_z, 6)],
        4: [(pages_over_z, 1), (pages_over_z, 7)],
        5: [(pages_over_y, 4)],
        6: [(pages_over_y, 3), (pages_over_y, 5)],
        7: [(pages_over_y, 2), (pages_over_y, 6)],
        8: [(pages_over_y, 1), (pages_over_y, 7)],
    }
    order = (0, 1, 3, 2)
    for tick in range(1, 9):
        for at, a in enumerate(order):
            k = tick - at
            if k == 0:
                start_chain(a)
            elif 1 <= k <= 4:
                advance(a, k)
        for action, d in extra[tick]:
            action(d)
        if tick == 4:
            send_weight()
    for copy in local:
        copy.wait()
    own_pages = []
    for at, a in enumerate((0, 1, 3, 2)):
        ys = (y + 4 - a) % Y
        held = by_y if a else by_z
        for d in range(Z):
            if a:
                page_y[d, a].wait_recv()
        to_core.append(send(held.at[:, ys, 1 - c], page_out.at[:, ys, c], across))
        copy = pltpu.make_async_copy(
            held.at[:, ys, c], page_out.at[:, ys, c], local_sem.at[3 + at]
        )
        copy.start()
        own_pages.append(copy)
    for a in (1, 3, 2):
        slot = (y + a) % Y * 2 + c
        near_w[a].wait_recv()
        to_core.append(send(w_all.at[slot], w_all.at[slot], across))
    for copy in to_core:
        copy.wait_recv()
    for copy in pending:
        copy.wait_send()
    for copy in own_pages:
        copy.wait()


def gather_blocks(kv_block, w_block, pages, seq_count):
    sems = 128
    return pl.pallas_call(
        gather_kernel,
        name="gather_blocks",
        out_shape=(
            jax.ShapeDtypeStruct((seq_count,) + kv_block.shape, kv_block.dtype),
            jax.ShapeDtypeStruct((2 * Y,) + w_block.shape, w_block.dtype),
            jax.ShapeDtypeStruct(pages.shape, pages.dtype),
        ),
        in_specs=[pl.BlockSpec(memory_space=pltpu.VMEM)] * 3,
        out_specs=[pl.BlockSpec(memory_space=pl.ANY)] * 2
        + [pl.BlockSpec(memory_space=pltpu.VMEM)],
        scratch_shapes=[
            pltpu.VMEM(pages.shape, pages.dtype),
            pltpu.VMEM(pages.shape, pages.dtype),
            pltpu.SemaphoreType.DMA((sems,)),
            pltpu.SemaphoreType.DMA((sems,)),
            pltpu.SemaphoreType.DMA((7,)),
        ],
        compiler_params=pltpu.CompilerParams(collective_id=0, has_side_effects=True),
    )(kv_block, w_block, pages)


def ring_kernel(x_ref, all_ref, send_sem, recv_sem, local_sem):
    me = lax.axis_index("seq")
    z, y, c = me // 8, (me // 2) % 4, me % 2
    rows = x_ref.shape[0]
    half = rows // 2
    up, down = seq_id((z + 1) % Z, y, c), seq_id((z + 7) % Z, y, c)
    meet([up, down])
    pending = []
    ring = {}

    def send(src, dst, device, direction, k):
        i = 2 * (k - 1) + (direction > 0)
        copy = pltpu.make_async_remote_copy(
            src_ref=src,
            dst_ref=dst,
            send_sem=send_sem.at[i],
            recv_sem=recv_sem.at[i],
            device_id={"seq": device},
            device_id_type=MESH,
        )
        copy.start()
        pending.append(copy)
        ring[direction, k] = copy

    send(x_ref, all_ref.at[z], up, 1, 1)
    send(x_ref, all_ref.at[z], down, -1, 1)
    local = pltpu.make_async_copy(x_ref, all_ref.at[z], local_sem)
    local.start()
    for k in (1, 2, 3, 4):
        for direction, target in ((1, up), (-1, down)):
            ring[direction, k].wait_recv()
            if k < 4:
                block = all_ref.at[(z + 8 - direction * k) % Z]
                if k == 3:
                    block = block.at[pl.ds(0, half)] if direction == 1 else block.at[pl.ds(half, half)]
                send(block, block, target, direction, k + 1)
    for copy in pending:
        copy.wait_send()
    local.wait()


def ring_gather(x):
    return pl.pallas_call(
        ring_kernel,
        name="ring_gather",
        out_shape=jax.ShapeDtypeStruct((Z,) + x.shape, x.dtype),
        in_specs=[pl.BlockSpec(memory_space=pltpu.VMEM)],
        out_specs=pl.BlockSpec(memory_space=pl.ANY),
        scratch_shapes=[
            pltpu.SemaphoreType.DMA((8,)),
            pltpu.SemaphoreType.DMA((8,)),
            pltpu.SemaphoreType.DMA,
        ],
        compiler_params=pltpu.CompilerParams(collective_id=1, has_side_effects=True),
    )(x)


def attention_kernel(q_ref, seg_ref, kv_ref, out_ref, qt_ref, top_ref, sum_ref, acc_ref):
    seq_place = lax.axis_index("seq")
    tokens = q_ref.shape[0]
    groups = q_ref.shape[1] // HEAD_SIZE
    span = KEY_BLOCKS * tokens
    factor = HEAD_SIZE ** (-0.5) * 1.4426950408889634
    table = jnp.sum(kv_ref[:, 2 * tokens :, :].astype(jnp.float32), axis=0)
    ids = lax.broadcasted_iota(jnp.int32, table.shape, 0)
    first = jnp.sum(jnp.where(ids == seg_ref[...], table, 0.0), axis=0, keepdims=True)
    lowest = jnp.min(first).astype(jnp.int32)
    highest = jnp.max(first).astype(jnp.int32)
    start = jnp.concatenate([first.astype(jnp.int32)] * groups, axis=1)
    place = lax.broadcasted_iota(jnp.int32, (1, tokens), 1) + seq_place * tokens
    place = jnp.concatenate([place] * groups, axis=1)
    for g in range(groups):
        qt_ref[g * tokens : (g + 1) * tokens, :] = q_ref[:, g * HEAD_SIZE : (g + 1) * HEAD_SIZE]
    top_ref[...] = jnp.full(top_ref.shape, -1e29, jnp.float32)
    sum_ref[...] = jnp.zeros(sum_ref.shape, jnp.float32)
    acc_ref[...] = jnp.zeros(acc_ref.shape, jnp.float32)

    def step(masked, i, carry):
        blocks = pl.ds(i * KEY_BLOCKS, KEY_BLOCKS)
        keys = kv_ref[blocks, 0:tokens, :].reshape(span, HEAD_SIZE)
        values = kv_ref[blocks, tokens : 2 * tokens, :].reshape(span, HEAD_SIZE)
        scores = lax.dot_general(
            keys, qt_ref[...], (((1,), (1,)), ((), ())), preferred_element_type=jnp.float32
        )
        if masked:
            key_place = lax.broadcasted_iota(jnp.int32, scores.shape, 0) + i * span
            allowed = (key_place >= start) & (key_place <= place)
            scores = jnp.where(allowed, scores, -1e30)
        old = top_ref[...]
        top = jnp.maximum(old, jnp.max(scores, axis=0, keepdims=True))
        weights = jnp.exp2((scores - top) * factor)
        shrink = jnp.exp2((old - top) * factor)
        top_ref[...] = top
        sum_ref[...] = sum_ref[...] * shrink + jnp.sum(weights, axis=0, keepdims=True)
        acc_ref[...] = acc_ref[...] * shrink + lax.dot_general(
            values,
            weights.astype(jnp.bfloat16),
            (((0,), (0,)), ((), ())),
            preferred_element_type=jnp.float32,
        )
        return carry

    begin = lowest // span
    end = (seq_place * tokens + tokens - 1) // span + 1
    clear_begin = jnp.minimum((highest + span - 1) // span, end)
    clear_end = jnp.maximum((seq_place * tokens + 1) // span, clear_begin)
    lax.fori_loop(begin, clear_begin, functools.partial(step, True), 0)
    lax.fori_loop(clear_begin, clear_end, functools.partial(step, False), 0)
    lax.fori_loop(clear_end, end, functools.partial(step, True), 0)
    result = acc_ref[...] / sum_ref[...]
    for g in range(groups):
        columns = slice(g * tokens, (g + 1) * tokens)
        out_ref[:, g * HEAD_SIZE : (g + 1) * HEAD_SIZE] = result[:, columns].T.astype(out_ref.dtype)


def attend(queries, segments, kv_all):
    tokens, width = queries.shape
    count = tokens * (width // HEAD_SIZE)
    return pl.pallas_call(
        attention_kernel,
        name="attend",
        out_shape=jax.ShapeDtypeStruct(queries.shape, queries.dtype),
        in_specs=[pl.BlockSpec(memory_space=pltpu.VMEM)] * 3,
        out_specs=pl.BlockSpec(memory_space=pltpu.VMEM),
        scratch_shapes=[
            pltpu.VMEM((count, HEAD_SIZE), jnp.bfloat16),
            pltpu.VMEM((1, count), jnp.float32),
            pltpu.VMEM((1, count), jnp.float32),
            pltpu.VMEM((HEAD_SIZE, count), jnp.float32),
        ],
    )(queries, segments, kv_all)


def on_device(
    block_query_rows,
    block_key_rows,
    block_value_rows,
    stretch_segments,
    residual,
    out_weight,
    cache_by_prefill,
    request_pages,
    request_owner,
):
    seq_count = lax.axis_size("seq")
    head_count = lax.axis_size("head")
    seq_place = lax.axis_index("seq")
    local_pages = cache_by_prefill.shape[2]
    capacity = 2 * local_pages
    per_pair = capacity // seq_count
    owners = jnp.arange(seq_count, dtype=jnp.int32)
    run_pages = jnp.sum(
        jnp.where(request_owner[None, :] == owners[:, None], request_pages[None, :], 0), axis=1
    )
    run_start = jnp.sum(
        jnp.where(request_owner[None, :] < owners[:, None], request_pages[None, :], 0), axis=1
    )
    pair_slots = jnp.arange(per_pair, dtype=jnp.int32)
    offset = (seq_place - run_start) % seq_count
    slot_index = pair_slots[None, :] * seq_count + offset[:, None]
    sending = slot_index < run_pages[:, None]
    local_index = pair_slots[None, :] + ((run_start + offset - seq_place) // seq_count)[:, None]
    local_index = jnp.where(sending, local_index, 0).reshape(-1)
    picked = jnp.take(cache_by_prefill, local_index, axis=2)
    outgoing = jnp.where(
        sending.reshape(-1)[None, None, :, None, None], picked, jnp.zeros_like(picked)
    )
    pages = jnp.moveaxis(outgoing, 2, 0)
    ids = jnp.arange(REQUESTS, dtype=jnp.int32)
    before = jnp.sum((stretch_segments[None, :] < ids[:, None]).astype(jnp.float32), axis=1)
    table = jnp.broadcast_to(before[:, None], (REQUESTS, HEAD_SIZE)).astype(jnp.bfloat16)
    kv_block = jnp.concatenate([block_key_rows, block_value_rows, table], axis=0)
    kv_all, w_all, moved = gather_blocks(
        kv_block, out_weight.T, pages.reshape(Z, Y, 2, -1, HEAD_SIZE), seq_count
    )
    incoming = jnp.moveaxis(moved.reshape(pages.shape), 0, 2)
    attention = attend(block_query_rows, stretch_segments[None, :], kv_all)
    attention_all = ring_gather(attention)
    rows, width = attention.shape
    partial_sums = lax.dot_general(
        attention_all.reshape(Z * rows, width),
        w_all.reshape(width, width),
        (((1,), (1,)), ((), ())),
        preferred_element_type=jnp.float32,
    ).astype(jnp.bfloat16)
    parts = lax.all_to_all(
        partial_sums.reshape(Z, rows, width), "head", split_axis=0, concat_axis=0, tiled=True
    )
    total = jnp.sum(parts.astype(jnp.float32), axis=0).astype(jnp.bfloat16)
    pairs = [
        ((z * 8 + rest) * head_count + h, (h * 8 + rest) * head_count + z)
        for z in range(Z)
        for rest in range(8)
        for h in range(head_count)
    ]
    mine = lax.ppermute(total, ("seq", "head"), pairs)
    layer_out = (residual.astype(jnp.float32) + mine.astype(jnp.float32)).astype(jnp.bfloat16)
    layers, pair_kv, _, page_len, width = incoming.shape
    arranged = jnp.swapaxes(
        incoming.reshape(layers, pair_kv, seq_count, per_pair, page_len, width), 2, 3
    )
    my_start = run_start[seq_place]
    my_pages = run_pages[seq_place]
    rotated = jnp.roll(arranged, -my_start, axis=3).reshape(
        layers, pair_kv, capacity, page_len, width
    )
    keep = jnp.arange(capacity, dtype=jnp.int32) < my_pages
    cache_decode = jnp.where(keep[None, None, :, None, None], rotated, jnp.zeros_like(rotated))
    return (layer_out, cache_decode)


def solution(mesh):
    return jax.shard_map(
        on_device,
        mesh=mesh,
        in_specs=(
            P("seq", "head"),
            P("seq", "head"),
            P("seq", "head"),
            P("seq"),
            P("seq", "head"),
            P("head", "seq"),
            P(None, None, "seq", None, "head"),
            P(),
            P(),
        ),
        out_specs=(P("seq", "head"), P(None, None, "seq", None, "head")),
        check_vma=False,
    )
```

```python
import functools

import jax
import jax.numpy as jnp
from jax import lax
from jax.experimental import pallas as pl
from jax.experimental.pallas import tpu as pltpu
from jax.sharding import PartitionSpec as P

HEAD_SIZE = 128
Z = 8
Y = 4
REQUESTS = 16
MESH = pl.DeviceIdType.MESH
KEY_BLOCKS = 8


def seq_id(z, y, c):
    return z * 8 + y * 2 + c


def meet(partners):
    barrier = pltpu.get_barrier_semaphore()
    for seq in partners:
        pl.semaphore_signal(barrier, inc=1, device_id={"seq": seq}, device_id_type=MESH)
    pl.semaphore_wait(barrier, len(partners))


def gather_kernel(kv_ref, w_ref, kv_all, w_all, send_sem, recv_sem, local_sem):
    me = lax.axis_index("seq")
    z, y, c = me // 8, (me // 2) % 4, me % 2
    rows = kv_ref.shape[0]
    cut = 144
    across = seq_id(z, y, 1 - c)
    up, down = seq_id((z + 1) % Z, y, c), seq_id((z + 7) % Z, y, c)
    meet([across, up, down] + [seq_id(z, (y + a) % Y, c) for a in (1, 3)])

    used = [0]
    pending = []

    def send(src, dst, device):
        i = used[0]
        used[0] += 1
        copy = pltpu.make_async_remote_copy(
            src_ref=src,
            dst_ref=dst,
            send_sem=send_sem.at[i],
            recv_sem=recv_sem.at[i],
            device_id={"seq": device},
            device_id_type=MESH,
        )
        copy.start()
        pending.append(copy)
        return copy

    def kv_at(seq, part):
        lo, hi = part
        return kv_all.at[seq, pl.ds(lo, hi - lo)]

    whole = (0, rows)
    to_core = []
    own_kv = kv_all.at[me]
    ring = {}
    ring[0, 1, 1] = send(kv_ref, own_kv, up)
    ring[0, -1, 1] = send(kv_ref, own_kv, down)
    near = {}
    left, right = seq_id(z, (y + 3) % Y, c), seq_id(z, (y + 1) % Y, c)
    near[1] = [send(kv_ref, own_kv, left)]
    near[3] = [send(kv_ref, own_kv, right)]
    near[2] = []
    to_core.append(send(kv_ref, own_kv, across))
    w_slot = y * 2 + c
    local = [
        pltpu.make_async_copy(kv_ref, own_kv, local_sem.at[0]),
        pltpu.make_async_copy(w_ref, w_all.at[w_slot], local_sem.at[1]),
    ]
    for copy in local:
        copy.start()

    def start_chain(a):
        seq = seq_id(z, (y + a) % Y, c)
        for copy in near[a]:
            copy.wait_recv()
        block = kv_at(seq, whole)
        if a == 1:
            half = kv_at(seq, (0, cut))
            near[2].append(send(half, half, left))
        if a == 3:
            half = kv_at(seq, (cut, rows))
            near[2].append(send(half, half, right))
        ring[a, 1, 1] = send(block, block, up)
        ring[a, -1, 1] = send(block, block, down)
        to_core.append(send(block, block, across))

    def advance(a, k):
        for direction, target in ((1, up), (-1, down)):
            seq = seq_id((z + 8 - direction * k) % Z, (y + a) % Y, c)
            ring[a, direction, k].wait_recv()
            part = whole
            if k == 4:
                part = (0, cut) if direction == 1 else (cut, rows)
            block = kv_at(seq, part)
            if k < 4:
                onward = block
                if k == 3:
                    onward = kv_at(seq, (0, cut) if direction == 1 else (cut, rows))
                ring[a, direction, k + 1] = send(onward, onward, target)
            to_core.append(send(block, block, across))

    near_w = {2: []}

    def send_weight():
        mine = w_all.at[w_slot]
        near_w[1] = [send(w_ref, mine, left)]
        near_w[3] = [send(w_ref, mine, right)]
        to_core.append(send(w_ref, mine, across))

    def weight_from(a):
        slot = (y + a) % Y * 2 + c
        block = w_all.at[slot]
        for copy in near_w[a]:
            copy.wait_recv()
        if a == 1:
            half = block.at[pl.ds(0, 48)]
            near_w[2].append(send(half, half, left))
        if a == 3:
            half = block.at[pl.ds(48, 32)]
            near_w[2].append(send(half, half, right))
        to_core.append(send(block, block, across))

    delay = {0: 0, 1: 1, 3: 1, 2: 3}
    for tick in range(1, 8):
        for a, late in delay.items():
            k = tick - late
            if k == 0:
                start_chain(a)
            elif 1 <= k <= 4:
                advance(a, k)
        if tick == 1:
            send_weight()
        if tick == 4:
            weight_from(1)
            weight_from(3)
    weight_from(2)
    for copy in to_core:
        copy.wait_recv()
    for copy in pending:
        copy.wait_send()
    for copy in local:
        copy.wait()


def gather_blocks(kv_block, w_block, seq_count):
    sems = 84
    return pl.pallas_call(
        gather_kernel,
        name="gather_blocks",
        out_shape=(
            jax.ShapeDtypeStruct((seq_count,) + kv_block.shape, kv_block.dtype),
            jax.ShapeDtypeStruct((2 * Y,) + w_block.shape, w_block.dtype),
        ),
        in_specs=[pl.BlockSpec(memory_space=pltpu.VMEM)] * 2,
        out_specs=[pl.BlockSpec(memory_space=pl.ANY)] * 2,
        scratch_shapes=[
            pltpu.SemaphoreType.DMA((sems,)),
            pltpu.SemaphoreType.DMA((sems,)),
            pltpu.SemaphoreType.DMA((2,)),
        ],
        compiler_params=pltpu.CompilerParams(collective_id=0, has_side_effects=True),
    )(kv_block, w_block)


def ring_kernel(x_ref, all_ref, send_sem, recv_sem, local_sem):
    me = lax.axis_index("seq")
    z, y, c = me // 8, (me // 2) % 4, me % 2
    rows = x_ref.shape[0]
    half = rows // 2
    up, down = seq_id((z + 1) % Z, y, c), seq_id((z + 7) % Z, y, c)
    meet([up, down])
    pending = []
    ring = {}

    def send(src, dst, device, direction, k):
        i = 2 * (k - 1) + (direction > 0)
        copy = pltpu.make_async_remote_copy(
            src_ref=src,
            dst_ref=dst,
            send_sem=send_sem.at[i],
            recv_sem=recv_sem.at[i],
            device_id={"seq": device},
            device_id_type=MESH,
        )
        copy.start()
        pending.append(copy)
        ring[direction, k] = copy

    send(x_ref, all_ref.at[z], up, 1, 1)
    send(x_ref, all_ref.at[z], down, -1, 1)
    local = pltpu.make_async_copy(x_ref, all_ref.at[z], local_sem)
    local.start()
    for k in (1, 2, 3, 4):
        for direction, target in ((1, up), (-1, down)):
            ring[direction, k].wait_recv()
            if k < 4:
                block = all_ref.at[(z + 8 - direction * k) % Z]
                if k == 3:
                    block = block.at[pl.ds(0, half)] if direction == 1 else block.at[pl.ds(half, half)]
                send(block, block, target, direction, k + 1)
    for copy in pending:
        copy.wait_send()
    local.wait()


def ring_gather(x):
    return pl.pallas_call(
        ring_kernel,
        name="ring_gather",
        out_shape=jax.ShapeDtypeStruct((Z,) + x.shape, x.dtype),
        in_specs=[pl.BlockSpec(memory_space=pltpu.VMEM)],
        out_specs=pl.BlockSpec(memory_space=pl.ANY),
        scratch_shapes=[
            pltpu.SemaphoreType.DMA((8,)),
            pltpu.SemaphoreType.DMA((8,)),
            pltpu.SemaphoreType.DMA,
        ],
        compiler_params=pltpu.CompilerParams(collective_id=1, has_side_effects=True),
    )(x)


def attention_kernel(q_ref, seg_ref, kv_ref, out_ref, qt_ref, top_ref, sum_ref, acc_ref):
    seq_place = lax.axis_index("seq")
    tokens = q_ref.shape[0]
    groups = q_ref.shape[1] // HEAD_SIZE
    span = KEY_BLOCKS * tokens
    factor = HEAD_SIZE ** (-0.5) * 1.4426950408889634
    table = jnp.sum(kv_ref[:, 2 * tokens :, :].astype(jnp.float32), axis=0)
    ids = lax.broadcasted_iota(jnp.int32, table.shape, 0)
    first = jnp.sum(jnp.where(ids == seg_ref[...], table, 0.0), axis=0, keepdims=True)
    lowest = jnp.min(first).astype(jnp.int32)
    highest = jnp.max(first).astype(jnp.int32)
    start = jnp.concatenate([first.astype(jnp.int32)] * groups, axis=1)
    place = lax.broadcasted_iota(jnp.int32, (1, tokens), 1) + seq_place * tokens
    place = jnp.concatenate([place] * groups, axis=1)
    for g in range(groups):
        qt_ref[g * tokens : (g + 1) * tokens, :] = q_ref[:, g * HEAD_SIZE : (g + 1) * HEAD_SIZE]
    top_ref[...] = jnp.full(top_ref.shape, -1e29, jnp.float32)
    sum_ref[...] = jnp.zeros(sum_ref.shape, jnp.float32)
    acc_ref[...] = jnp.zeros(acc_ref.shape, jnp.float32)

    def step(masked, i, carry):
        blocks = pl.ds(i * KEY_BLOCKS, KEY_BLOCKS)
        keys = kv_ref[blocks, 0:tokens, :].reshape(span, HEAD_SIZE)
        values = kv_ref[blocks, tokens : 2 * tokens, :].reshape(span, HEAD_SIZE)
        scores = lax.dot_general(
            keys, qt_ref[...], (((1,), (1,)), ((), ())), preferred_element_type=jnp.float32
        )
        if masked:
            key_place = lax.broadcasted_iota(jnp.int32, scores.shape, 0) + i * span
            allowed = (key_place >= start) & (key_place <= place)
            scores = jnp.where(allowed, scores, -1e30)
        old = top_ref[...]
        top = jnp.maximum(old, jnp.max(scores, axis=0, keepdims=True))
        weights = jnp.exp2((scores - top) * factor)
        shrink = jnp.exp2((old - top) * factor)
        top_ref[...] = top
        sum_ref[...] = sum_ref[...] * shrink + jnp.sum(weights, axis=0, keepdims=True)
        acc_ref[...] = acc_ref[...] * shrink + lax.dot_general(
            values,
            weights.astype(jnp.bfloat16),
            (((0,), (0,)), ((), ())),
            preferred_element_type=jnp.float32,
        )
        return carry

    begin = lowest // span
    end = (seq_place * tokens + tokens - 1) // span + 1
    clear_begin = jnp.minimum((highest + span - 1) // span, end)
    clear_end = jnp.maximum((seq_place * tokens + 1) // span, clear_begin)
    lax.fori_loop(begin, clear_begin, functools.partial(step, True), 0)
    lax.fori_loop(clear_begin, clear_end, functools.partial(step, False), 0)
    lax.fori_loop(clear_end, end, functools.partial(step, True), 0)
    result = acc_ref[...] / sum_ref[...]
    for g in range(groups):
        columns = slice(g * tokens, (g + 1) * tokens)
        out_ref[:, g * HEAD_SIZE : (g + 1) * HEAD_SIZE] = result[:, columns].T.astype(out_ref.dtype)


def attend(queries, segments, kv_all):
    tokens, width = queries.shape
    count = tokens * (width // HEAD_SIZE)
    return pl.pallas_call(
        attention_kernel,
        name="attend",
        out_shape=jax.ShapeDtypeStruct(queries.shape, queries.dtype),
        in_specs=[pl.BlockSpec(memory_space=pltpu.VMEM)] * 3,
        out_specs=pl.BlockSpec(memory_space=pltpu.VMEM),
        scratch_shapes=[
            pltpu.VMEM((count, HEAD_SIZE), jnp.bfloat16),
            pltpu.VMEM((1, count), jnp.float32),
            pltpu.VMEM((1, count), jnp.float32),
            pltpu.VMEM((HEAD_SIZE, count), jnp.float32),
        ],
        cost_estimate=pl.CostEstimate(flops=0, bytes_accessed=100_000_000, transcendentals=0),
    )(queries, segments, kv_all)


def on_device(
    block_query_rows,
    block_key_rows,
    block_value_rows,
    stretch_segments,
    residual,
    out_weight,
    cache_by_prefill,
    request_pages,
    request_owner,
):
    seq_count = lax.axis_size("seq")
    head_count = lax.axis_size("head")
    seq_place = lax.axis_index("seq")
    ids = jnp.arange(REQUESTS, dtype=jnp.int32)
    before = jnp.sum((stretch_segments[None, :] < ids[:, None]).astype(jnp.float32), axis=1)
    table = jnp.broadcast_to(before[:, None], (REQUESTS, HEAD_SIZE)).astype(jnp.bfloat16)
    kv_block = jnp.concatenate([block_key_rows, block_value_rows, table], axis=0)
    kv_all, w_all = gather_blocks(kv_block, out_weight.T, seq_count)
    local_pages = cache_by_prefill.shape[2]
    capacity = 2 * local_pages
    per_pair = capacity // seq_count
    owners = jnp.arange(seq_count, dtype=jnp.int32)
    run_pages = jnp.sum(
        jnp.where(request_owner[None, :] == owners[:, None], request_pages[None, :], 0), axis=1
    )
    run_start = jnp.sum(
        jnp.where(request_owner[None, :] < owners[:, None], request_pages[None, :], 0), axis=1
    )
    pair_slots = jnp.arange(per_pair, dtype=jnp.int32)
    offset = (seq_place - run_start) % seq_count
    slot_index = pair_slots[None, :] * seq_count + offset[:, None]
    sending = slot_index < run_pages[:, None]
    local_index = pair_slots[None, :] + ((run_start + offset - seq_place) // seq_count)[:, None]
    local_index = jnp.where(sending, local_index, 0).reshape(-1)
    picked = jnp.take(cache_by_prefill, local_index, axis=2)
    outgoing = jnp.where(
        sending.reshape(-1)[None, None, :, None, None], picked, jnp.zeros_like(picked)
    )
    outgoing, kv_all = lax.optimization_barrier((outgoing, kv_all))
    incoming = lax.all_to_all(outgoing, "seq", split_axis=2, concat_axis=2, tiled=True)
    attention = attend(block_query_rows, stretch_segments[None, :], kv_all)
    attention_all = ring_gather(attention)
    attention_all, incoming = lax.optimization_barrier((attention_all, incoming))
    rows, width = attention.shape
    partial_sums = lax.dot_general(
        attention_all.reshape(Z * rows, width),
        w_all.reshape(width, width),
        (((1,), (1,)), ((), ())),
        preferred_element_type=jnp.float32,
    ).astype(jnp.bfloat16)
    parts = lax.all_to_all(
        partial_sums.reshape(Z, rows, width), "head", split_axis=0, concat_axis=0, tiled=True
    )
    total = jnp.sum(parts.astype(jnp.float32), axis=0).astype(jnp.bfloat16)
    pairs = [
        ((z * 8 + rest) * head_count + h, (h * 8 + rest) * head_count + z)
        for z in range(Z)
        for rest in range(8)
        for h in range(head_count)
    ]
    mine = lax.ppermute(total, ("seq", "head"), pairs)
    layer_out = (residual.astype(jnp.float32) + mine.astype(jnp.float32)).astype(jnp.bfloat16)
    layers, pair_kv, _, page_len, width = incoming.shape
    arranged = jnp.swapaxes(
        incoming.reshape(layers, pair_kv, seq_count, per_pair, page_len, width), 2, 3
    )
    my_start = run_start[seq_place]
    my_pages = run_pages[seq_place]
    rotated = jnp.roll(arranged, -my_start, axis=3).reshape(
        layers, pair_kv, capacity, page_len, width
    )
    keep = jnp.arange(capacity, dtype=jnp.int32) < my_pages
    cache_decode = jnp.where(keep[None, None, :, None, None], rotated, jnp.zeros_like(rotated))
    return (layer_out, cache_decode)


def solution(mesh):
    return jax.shard_map(
        on_device,
        mesh=mesh,
        in_specs=(
            P("seq", "head"),
            P("seq", "head"),
            P("seq", "head"),
            P("seq"),
            P("seq", "head"),
            P("head", "seq"),
            P(None, None, "seq", None, "head"),
            P(),
            P(),
        ),
        out_specs=(P("seq", "head"), P(None, None, "seq", None, "head")),
        check_vma=False,
    )
```

```python
import functools

import jax
import jax.numpy as jnp
from jax import lax
from jax.experimental import pallas as pl
from jax.experimental.pallas import tpu as pltpu
from jax.sharding import PartitionSpec as P

HEAD_SIZE = 128
Z = 8
Y = 4
REQUESTS = 16
MESH = pl.DeviceIdType.MESH
KEY_BLOCKS = 8


def seq_id(z, y, c):
    return z * 8 + y * 2 + c


def meet(partners):
    barrier = pltpu.get_barrier_semaphore()
    for seq in partners:
        pl.semaphore_signal(barrier, inc=1, device_id={"seq": seq}, device_id_type=MESH)
    pl.semaphore_wait(barrier, len(partners))


def gather_kernel(kv_ref, w_ref, kv_all, w_all, send_sem, recv_sem, local_sem):
    me = lax.axis_index("seq")
    z, y, c = me // 8, (me // 2) % 4, me % 2
    rows = kv_ref.shape[0]
    cut = 144
    across = seq_id(z, y, 1 - c)
    up, down = seq_id((z + 1) % Z, y, c), seq_id((z + 7) % Z, y, c)
    meet([across, up, down] + [seq_id(z, (y + a) % Y, c) for a in (1, 3)])

    used = [0]
    pending = []

    def send(src, dst, device):
        i = used[0]
        used[0] += 1
        copy = pltpu.make_async_remote_copy(
            src_ref=src,
            dst_ref=dst,
            send_sem=send_sem.at[i],
            recv_sem=recv_sem.at[i],
            device_id={"seq": device},
            device_id_type=MESH,
        )
        copy.start()
        pending.append(copy)
        return copy

    def kv_at(seq, part):
        lo, hi = part
        return kv_all.at[seq, pl.ds(lo, hi - lo)]

    whole = (0, rows)
    to_core = []
    own_kv = kv_all.at[me]
    ring = {}
    ring[0, 1, 1] = send(kv_ref, own_kv, up)
    ring[0, -1, 1] = send(kv_ref, own_kv, down)
    near = {}
    left, right = seq_id(z, (y + 3) % Y, c), seq_id(z, (y + 1) % Y, c)
    near[1] = [send(kv_ref, own_kv, left)]
    near[3] = [send(kv_ref, own_kv, right)]
    near[2] = []
    to_core.append(send(kv_ref, own_kv, across))
    w_slot = y * 2 + c
    local = [
        pltpu.make_async_copy(kv_ref, own_kv, local_sem.at[0]),
        pltpu.make_async_copy(w_ref, w_all.at[w_slot], local_sem.at[1]),
    ]
    for copy in local:
        copy.start()

    def start_chain(a):
        seq = seq_id(z, (y + a) % Y, c)
        for copy in near[a]:
            copy.wait_recv()
        block = kv_at(seq, whole)
        if a == 1:
            half = kv_at(seq, (0, cut))
            near[2].append(send(half, half, left))
        if a == 3:
            half = kv_at(seq, (cut, rows))
            near[2].append(send(half, half, right))
        ring[a, 1, 1] = send(block, block, up)
        ring[a, -1, 1] = send(block, block, down)
        to_core.append(send(block, block, across))

    def advance(a, k):
        for direction, target in ((1, up), (-1, down)):
            seq = seq_id((z + 8 - direction * k) % Z, (y + a) % Y, c)
            ring[a, direction, k].wait_recv()
            part = whole
            if k == 4:
                part = (0, cut) if direction == 1 else (cut, rows)
            block = kv_at(seq, part)
            if k < 4:
                onward = block
                if k == 3:
                    onward = kv_at(seq, (0, cut) if direction == 1 else (cut, rows))
                ring[a, direction, k + 1] = send(onward, onward, target)
            to_core.append(send(block, block, across))

    near_w = {2: []}

    def send_weight():
        mine = w_all.at[w_slot]
        near_w[1] = [send(w_ref, mine, left)]
        near_w[3] = [send(w_ref, mine, right)]
        to_core.append(send(w_ref, mine, across))

    def weight_from(a):
        slot = (y + a) % Y * 2 + c
        block = w_all.at[slot]
        for copy in near_w[a]:
            copy.wait_recv()
        if a == 1:
            half = block.at[pl.ds(0, 48)]
            near_w[2].append(send(half, half, left))
        if a == 3:
            half = block.at[pl.ds(48, 32)]
            near_w[2].append(send(half, half, right))
        to_core.append(send(block, block, across))

    delay = {0: 0, 1: 1, 3: 1, 2: 3}
    for tick in range(1, 8):
        for a, late in delay.items():
            k = tick - late
            if k == 0:
                start_chain(a)
            elif 1 <= k <= 4:
                advance(a, k)
        if tick == 1:
            send_weight()
        if tick == 4:
            weight_from(1)
            weight_from(3)
    weight_from(2)
    for copy in to_core:
        copy.wait_recv()
    for copy in pending:
        copy.wait_send()
    for copy in local:
        copy.wait()


def gather_blocks(kv_block, w_block, seq_count):
    sems = 84
    return pl.pallas_call(
        gather_kernel,
        name="gather_blocks",
        out_shape=(
            jax.ShapeDtypeStruct((seq_count,) + kv_block.shape, kv_block.dtype),
            jax.ShapeDtypeStruct((2 * Y,) + w_block.shape, w_block.dtype),
        ),
        in_specs=[pl.BlockSpec(memory_space=pltpu.VMEM)] * 2,
        out_specs=[pl.BlockSpec(memory_space=pl.ANY)] * 2,
        scratch_shapes=[
            pltpu.SemaphoreType.DMA((sems,)),
            pltpu.SemaphoreType.DMA((sems,)),
            pltpu.SemaphoreType.DMA((2,)),
        ],
        compiler_params=pltpu.CompilerParams(collective_id=0, has_side_effects=True),
    )(kv_block, w_block)


def ring_kernel(x_ref, all_ref, send_sem, recv_sem, local_sem):
    me = lax.axis_index("seq")
    z, y, c = me // 8, (me // 2) % 4, me % 2
    rows = x_ref.shape[0]
    half = rows // 2
    up, down = seq_id((z + 1) % Z, y, c), seq_id((z + 7) % Z, y, c)
    meet([up, down])
    pending = []
    ring = {}

    def send(src, dst, device, direction, k):
        i = 2 * (k - 1) + (direction > 0)
        copy = pltpu.make_async_remote_copy(
            src_ref=src,
            dst_ref=dst,
            send_sem=send_sem.at[i],
            recv_sem=recv_sem.at[i],
            device_id={"seq": device},
            device_id_type=MESH,
        )
        copy.start()
        pending.append(copy)
        ring[direction, k] = copy

    send(x_ref, all_ref.at[z], up, 1, 1)
    send(x_ref, all_ref.at[z], down, -1, 1)
    local = pltpu.make_async_copy(x_ref, all_ref.at[z], local_sem)
    local.start()
    for k in (1, 2, 3, 4):
        for direction, target in ((1, up), (-1, down)):
            ring[direction, k].wait_recv()
            if k < 4:
                block = all_ref.at[(z + 8 - direction * k) % Z]
                if k == 3:
                    block = block.at[pl.ds(0, half)] if direction == 1 else block.at[pl.ds(half, half)]
                send(block, block, target, direction, k + 1)
    for copy in pending:
        copy.wait_send()
    local.wait()


def ring_gather(x):
    return pl.pallas_call(
        ring_kernel,
        name="ring_gather",
        out_shape=jax.ShapeDtypeStruct((Z,) + x.shape, x.dtype),
        in_specs=[pl.BlockSpec(memory_space=pltpu.VMEM)],
        out_specs=pl.BlockSpec(memory_space=pl.ANY),
        scratch_shapes=[
            pltpu.SemaphoreType.DMA((8,)),
            pltpu.SemaphoreType.DMA((8,)),
            pltpu.SemaphoreType.DMA,
        ],
        compiler_params=pltpu.CompilerParams(collective_id=1, has_side_effects=True),
    )(x)


def head_sum_kernel(part_ref, out_ref, held, send_sem, recv_sem):
    place = lax.axis_index("head")
    count = part_ref.shape[0]
    barrier = pltpu.get_barrier_semaphore()
    for d in range(1, count):
        pl.semaphore_signal(
            barrier, inc=1, device_id={"head": (place + d) % count}, device_id_type=MESH
        )
    pl.semaphore_wait(barrier, count - 1)
    copies = {}
    for d in (4, 3, 5, 2, 6, 1, 7):
        to = (place + d) % count
        copies[d] = pltpu.make_async_remote_copy(
            src_ref=part_ref.at[to],
            dst_ref=held.at[place],
            send_sem=send_sem.at[d - 1],
            recv_sem=recv_sem.at[d - 1],
            device_id={"head": to},
            device_id_type=MESH,
        )
        copies[d].start()
    total = part_ref[place].astype(jnp.float32)
    for d in (1, 7, 2, 6, 3, 5, 4):
        copies[d].wait_recv()
        total = total + held[(place + count - d) % count].astype(jnp.float32)
    out_ref[...] = total.astype(out_ref.dtype)
    for copy in copies.values():
        copy.wait_send()


def head_sum(parts):
    return pl.pallas_call(
        head_sum_kernel,
        name="head_sum",
        out_shape=jax.ShapeDtypeStruct(parts.shape[1:], parts.dtype),
        in_specs=[pl.BlockSpec(memory_space=pltpu.VMEM)],
        out_specs=pl.BlockSpec(memory_space=pltpu.VMEM),
        scratch_shapes=[
            pltpu.VMEM(parts.shape, parts.dtype),
            pltpu.SemaphoreType.DMA((7,)),
            pltpu.SemaphoreType.DMA((7,)),
        ],
        cost_estimate=pl.CostEstimate(flops=0, bytes_accessed=100_000_000, transcendentals=0),
        compiler_params=pltpu.CompilerParams(collective_id=2, has_side_effects=True),
    )(parts)


def attention_kernel(q_ref, seg_ref, kv_ref, out_ref, qt_ref, top_ref, sum_ref, acc_ref):
    seq_place = lax.axis_index("seq")
    tokens = q_ref.shape[0]
    groups = q_ref.shape[1] // HEAD_SIZE
    span = KEY_BLOCKS * tokens
    factor = HEAD_SIZE ** (-0.5) * 1.4426950408889634
    table = jnp.sum(kv_ref[:, 2 * tokens :, :].astype(jnp.float32), axis=0)
    ids = lax.broadcasted_iota(jnp.int32, table.shape, 0)
    first = jnp.sum(jnp.where(ids == seg_ref[...], table, 0.0), axis=0, keepdims=True)
    lowest = jnp.min(first).astype(jnp.int32)
    highest = jnp.max(first).astype(jnp.int32)
    start = jnp.concatenate([first.astype(jnp.int32)] * groups, axis=1)
    place = lax.broadcasted_iota(jnp.int32, (1, tokens), 1) + seq_place * tokens
    place = jnp.concatenate([place] * groups, axis=1)
    for g in range(groups):
        qt_ref[g * tokens : (g + 1) * tokens, :] = q_ref[:, g * HEAD_SIZE : (g + 1) * HEAD_SIZE]
    top_ref[...] = jnp.full(top_ref.shape, -1e29, jnp.float32)
    sum_ref[...] = jnp.zeros(sum_ref.shape, jnp.float32)
    acc_ref[...] = jnp.zeros(acc_ref.shape, jnp.float32)

    def step(masked, i, carry):
        blocks = pl.ds(i * KEY_BLOCKS, KEY_BLOCKS)
        keys = kv_ref[blocks, 0:tokens, :].reshape(span, HEAD_SIZE)
        values = kv_ref[blocks, tokens : 2 * tokens, :].reshape(span, HEAD_SIZE)
        scores = lax.dot_general(
            keys, qt_ref[...], (((1,), (1,)), ((), ())), preferred_element_type=jnp.float32
        )
        if masked:
            key_place = lax.broadcasted_iota(jnp.int32, scores.shape, 0) + i * span
            allowed = (key_place >= start) & (key_place <= place)
            scores = jnp.where(allowed, scores, -1e30)
        old = top_ref[...]
        top = jnp.maximum(old, jnp.max(scores, axis=0, keepdims=True))
        weights = jnp.exp2((scores - top) * factor)
        shrink = jnp.exp2((old - top) * factor)
        top_ref[...] = top
        sum_ref[...] = sum_ref[...] * shrink + jnp.sum(weights, axis=0, keepdims=True)
        acc_ref[...] = acc_ref[...] * shrink + lax.dot_general(
            values,
            weights.astype(jnp.bfloat16),
            (((0,), (0,)), ((), ())),
            preferred_element_type=jnp.float32,
        )
        return carry

    begin = lowest // span
    end = (seq_place * tokens + tokens - 1) // span + 1
    clear_begin = jnp.minimum((highest + span - 1) // span, end)
    clear_end = jnp.maximum((seq_place * tokens + 1) // span, clear_begin)
    lax.fori_loop(begin, clear_begin, functools.partial(step, True), 0)
    lax.fori_loop(clear_begin, clear_end, functools.partial(step, False), 0)
    lax.fori_loop(clear_end, end, functools.partial(step, True), 0)
    result = acc_ref[...] / sum_ref[...]
    for g in range(groups):
        columns = slice(g * tokens, (g + 1) * tokens)
        out_ref[:, g * HEAD_SIZE : (g + 1) * HEAD_SIZE] = result[:, columns].T.astype(out_ref.dtype)


def attend(queries, segments, kv_all):
    tokens, width = queries.shape
    count = tokens * (width // HEAD_SIZE)
    return pl.pallas_call(
        attention_kernel,
        name="attend",
        out_shape=jax.ShapeDtypeStruct(queries.shape, queries.dtype),
        in_specs=[pl.BlockSpec(memory_space=pltpu.VMEM)] * 3,
        out_specs=pl.BlockSpec(memory_space=pltpu.VMEM),
        scratch_shapes=[
            pltpu.VMEM((count, HEAD_SIZE), jnp.bfloat16),
            pltpu.VMEM((1, count), jnp.float32),
            pltpu.VMEM((1, count), jnp.float32),
            pltpu.VMEM((HEAD_SIZE, count), jnp.float32),
        ],
        cost_estimate=pl.CostEstimate(flops=0, bytes_accessed=100_000_000, transcendentals=0),
    )(queries, segments, kv_all)


def on_device(
    block_query_rows,
    block_key_rows,
    block_value_rows,
    stretch_segments,
    residual,
    out_weight,
    cache_by_prefill,
    request_pages,
    request_owner,
):
    seq_count = lax.axis_size("seq")
    head_count = lax.axis_size("head")
    seq_place = lax.axis_index("seq")
    ids = jnp.arange(REQUESTS, dtype=jnp.int32)
    before = jnp.sum((stretch_segments[None, :] < ids[:, None]).astype(jnp.float32), axis=1)
    table = jnp.broadcast_to(before[:, None], (REQUESTS, HEAD_SIZE)).astype(jnp.bfloat16)
    kv_block = jnp.concatenate([block_key_rows, block_value_rows, table], axis=0)
    kv_all, w_all = gather_blocks(kv_block, out_weight.T, seq_count)
    local_pages = cache_by_prefill.shape[2]
    capacity = 2 * local_pages
    per_pair = capacity // seq_count
    owners = jnp.arange(seq_count, dtype=jnp.int32)
    run_pages = jnp.sum(
        jnp.where(request_owner[None, :] == owners[:, None], request_pages[None, :], 0), axis=1
    )
    run_start = jnp.sum(
        jnp.where(request_owner[None, :] < owners[:, None], request_pages[None, :], 0), axis=1
    )
    pair_slots = jnp.arange(per_pair, dtype=jnp.int32)
    offset = (seq_place - run_start) % seq_count
    slot_index = pair_slots[None, :] * seq_count + offset[:, None]
    sending = slot_index < run_pages[:, None]
    local_index = pair_slots[None, :] + ((run_start + offset - seq_place) // seq_count)[:, None]
    local_index = jnp.where(sending, local_index, 0).reshape(-1)
    picked = jnp.take(cache_by_prefill, local_index, axis=2)
    outgoing = jnp.where(
        sending.reshape(-1)[None, None, :, None, None], picked, jnp.zeros_like(picked)
    )
    attention = attend(block_query_rows, stretch_segments[None, :], kv_all)
    attention_all = ring_gather(attention)
    outgoing, attention_all = lax.optimization_barrier((outgoing, attention_all))
    incoming = lax.all_to_all(outgoing, "seq", split_axis=2, concat_axis=2, tiled=True)
    rows, width = attention.shape
    partial_sums = lax.dot_general(
        attention_all.reshape(Z * rows, width),
        w_all.reshape(width, width),
        (((1,), (1,)), ((), ())),
        preferred_element_type=jnp.float32,
    ).astype(jnp.bfloat16)
    total = head_sum(partial_sums.reshape(Z, rows, width))
    pairs = [
        ((z * 8 + rest) * head_count + h, (h * 8 + rest) * head_count + z)
        for z in range(Z)
        for rest in range(8)
        for h in range(head_count)
    ]
    mine = lax.ppermute(total, ("seq", "head"), pairs)
    layer_out = (residual.astype(jnp.float32) + mine.astype(jnp.float32)).astype(jnp.bfloat16)
    layers, pair_kv, _, page_len, width = incoming.shape
    arranged = jnp.swapaxes(
        incoming.reshape(layers, pair_kv, seq_count, per_pair, page_len, width), 2, 3
    )
    my_start = run_start[seq_place]
    my_pages = run_pages[seq_place]
    rotated = jnp.roll(arranged, -my_start, axis=3).reshape(
        layers, pair_kv, capacity, page_len, width
    )
    keep = jnp.arange(capacity, dtype=jnp.int32) < my_pages
    cache_decode = jnp.where(keep[None, None, :, None, None], rotated, jnp.zeros_like(rotated))
    return (layer_out, cache_decode)


def solution(mesh):
    return jax.shard_map(
        on_device,
        mesh=mesh,
        in_specs=(
            P("seq", "head"),
            P("seq", "head"),
            P("seq", "head"),
            P("seq"),
            P("seq", "head"),
            P("head", "seq"),
            P(None, None, "seq", None, "head"),
            P(),
            P(),
        ),
        out_specs=(P("seq", "head"), P(None, None, "seq", None, "head")),
        check_vma=False,
    )
```

```python
import functools

import jax
import jax.numpy as jnp
from jax import lax
from jax.experimental import pallas as pl
from jax.experimental.pallas import tpu as pltpu
from jax.sharding import PartitionSpec as P

HEAD_SIZE = 128
Z = 8
Y = 4
REQUESTS = 16
MESH = pl.DeviceIdType.MESH
KEY_BLOCKS = 8


def seq_id(z, y, c):
    return z * 8 + y * 2 + c


def meet(partners):
    barrier = pltpu.get_barrier_semaphore()
    for seq in partners:
        pl.semaphore_signal(barrier, inc=1, device_id={"seq": seq}, device_id_type=MESH)
    pl.semaphore_wait(barrier, len(partners))


def gather_kernel(kv_ref, w_ref, kv_all, w_all, send_sem, recv_sem, local_sem):
    me = lax.axis_index("seq")
    z, y, c = me // 8, (me // 2) % 4, me % 2
    rows = kv_ref.shape[0]
    cut = 144
    across = seq_id(z, y, 1 - c)
    up, down = seq_id((z + 1) % Z, y, c), seq_id((z + 7) % Z, y, c)
    meet([across, up, down] + [seq_id(z, (y + a) % Y, c) for a in (1, 3)])

    used = [0]
    pending = []

    def send(src, dst, device):
        i = used[0]
        used[0] += 1
        copy = pltpu.make_async_remote_copy(
            src_ref=src,
            dst_ref=dst,
            send_sem=send_sem.at[i],
            recv_sem=recv_sem.at[i],
            device_id={"seq": device},
            device_id_type=MESH,
        )
        copy.start()
        pending.append(copy)
        return copy

    def kv_at(seq, part):
        lo, hi = part
        return kv_all.at[seq, pl.ds(lo, hi - lo)]

    whole = (0, rows)
    to_core = []
    own_kv = kv_all.at[me]
    ring = {}
    ring[0, 1, 1] = send(kv_ref, own_kv, up)
    ring[0, -1, 1] = send(kv_ref, own_kv, down)
    near = {}
    left, right = seq_id(z, (y + 3) % Y, c), seq_id(z, (y + 1) % Y, c)
    near[1] = [send(kv_ref, own_kv, left)]
    near[3] = [send(kv_ref, own_kv, right)]
    near[2] = []
    to_core.append(send(kv_ref, own_kv, across))
    w_slot = y * 2 + c
    local = [
        pltpu.make_async_copy(kv_ref, own_kv, local_sem.at[0]),
        pltpu.make_async_copy(w_ref, w_all.at[w_slot], local_sem.at[1]),
    ]
    for copy in local:
        copy.start()

    def start_chain(a):
        seq = seq_id(z, (y + a) % Y, c)
        for copy in near[a]:
            copy.wait_recv()
        block = kv_at(seq, whole)
        if a == 1:
            half = kv_at(seq, (0, cut))
            near[2].append(send(half, half, left))
        if a == 3:
            half = kv_at(seq, (cut, rows))
            near[2].append(send(half, half, right))
        ring[a, 1, 1] = send(block, block, up)
        ring[a, -1, 1] = send(block, block, down)
        to_core.append(send(block, block, across))

    def advance(a, k):
        for direction, target in ((1, up), (-1, down)):
            seq = seq_id((z + 8 - direction * k) % Z, (y + a) % Y, c)
            ring[a, direction, k].wait_recv()
            part = whole
            if k == 4:
                part = (0, cut) if direction == 1 else (cut, rows)
            block = kv_at(seq, part)
            if k < 4:
                onward = block
                if k == 3:
                    onward = kv_at(seq, (0, cut) if direction == 1 else (cut, rows))
                ring[a, direction, k + 1] = send(onward, onward, target)
            to_core.append(send(block, block, across))

    near_w = {2: []}

    def send_weight():
        mine = w_all.at[w_slot]
        near_w[1] = [send(w_ref, mine, left)]
        near_w[3] = [send(w_ref, mine, right)]
        to_core.append(send(w_ref, mine, across))

    def weight_from(a):
        slot = (y + a) % Y * 2 + c
        block = w_all.at[slot]
        for copy in near_w[a]:
            copy.wait_recv()
        if a == 1:
            half = block.at[pl.ds(0, 48)]
            near_w[2].append(send(half, half, left))
        if a == 3:
            half = block.at[pl.ds(48, 32)]
            near_w[2].append(send(half, half, right))
        to_core.append(send(block, block, across))

    delay = {0: 0, 1: 1, 3: 1, 2: 3}
    for tick in range(1, 8):
        for a, late in delay.items():
            k = tick - late
            if k == 0:
                start_chain(a)
            elif 1 <= k <= 4:
                advance(a, k)
        if tick == 1:
            send_weight()
        if tick == 4:
            weight_from(1)
            weight_from(3)
    weight_from(2)
    for copy in to_core:
        copy.wait_recv()
    for copy in pending:
        copy.wait_send()
    for copy in local:
        copy.wait()


def gather_blocks(kv_block, w_block, seq_count):
    sems = 84
    return pl.pallas_call(
        gather_kernel,
        name="gather_blocks",
        out_shape=(
            jax.ShapeDtypeStruct((seq_count,) + kv_block.shape, kv_block.dtype),
            jax.ShapeDtypeStruct((2 * Y,) + w_block.shape, w_block.dtype),
        ),
        in_specs=[pl.BlockSpec(memory_space=pltpu.VMEM)] * 2,
        out_specs=[pl.BlockSpec(memory_space=pl.ANY)] * 2,
        scratch_shapes=[
            pltpu.SemaphoreType.DMA((sems,)),
            pltpu.SemaphoreType.DMA((sems,)),
            pltpu.SemaphoreType.DMA((2,)),
        ],
        compiler_params=pltpu.CompilerParams(collective_id=0, has_side_effects=True),
    )(kv_block, w_block)


def ring_kernel(x_ref, all_ref, send_sem, recv_sem, local_sem):
    me = lax.axis_index("seq")
    z, y, c = me // 8, (me // 2) % 4, me % 2
    rows = x_ref.shape[0]
    half = rows // 2
    up, down = seq_id((z + 1) % Z, y, c), seq_id((z + 7) % Z, y, c)
    meet([up, down])
    pending = []
    ring = {}

    def send(src, dst, device, direction, k):
        i = 2 * (k - 1) + (direction > 0)
        copy = pltpu.make_async_remote_copy(
            src_ref=src,
            dst_ref=dst,
            send_sem=send_sem.at[i],
            recv_sem=recv_sem.at[i],
            device_id={"seq": device},
            device_id_type=MESH,
        )
        copy.start()
        pending.append(copy)
        ring[direction, k] = copy

    send(x_ref, all_ref.at[z], up, 1, 1)
    send(x_ref, all_ref.at[z], down, -1, 1)
    local = pltpu.make_async_copy(x_ref, all_ref.at[z], local_sem)
    local.start()
    for k in (1, 2, 3, 4):
        for direction, target in ((1, up), (-1, down)):
            ring[direction, k].wait_recv()
            if k < 4:
                block = all_ref.at[(z + 8 - direction * k) % Z]
                if k == 3:
                    block = block.at[pl.ds(0, half)] if direction == 1 else block.at[pl.ds(half, half)]
                send(block, block, target, direction, k + 1)
    for copy in pending:
        copy.wait_send()
    local.wait()


def ring_gather(x):
    return pl.pallas_call(
        ring_kernel,
        name="ring_gather",
        out_shape=jax.ShapeDtypeStruct((Z,) + x.shape, x.dtype),
        in_specs=[pl.BlockSpec(memory_space=pltpu.VMEM)],
        out_specs=pl.BlockSpec(memory_space=pl.ANY),
        scratch_shapes=[
            pltpu.SemaphoreType.DMA((8,)),
            pltpu.SemaphoreType.DMA((8,)),
            pltpu.SemaphoreType.DMA,
        ],
        compiler_params=pltpu.CompilerParams(collective_id=1, has_side_effects=True),
    )(x)


def head_sum_kernel(
    part_ref, residual_ref, out_ref, held, total_ref, arrived, send_sem, recv_sem, swap_sem
):
    me, place = lax.axis_index("seq"), lax.axis_index("head")
    z = me // 8
    count = part_ref.shape[0]
    mirror = {"seq": place * 8 + me % 8, "head": z}
    away = z != place
    barrier = pltpu.get_barrier_semaphore()
    for d in range(1, count):
        pl.semaphore_signal(
            barrier, inc=1, device_id={"head": (place + d) % count}, device_id_type=MESH
        )

    @pl.when(away)
    def _():
        pl.semaphore_signal(barrier, inc=1, device_id=mirror, device_id_type=MESH)
        pl.semaphore_wait(barrier, count)

    @pl.when(jnp.logical_not(away))
    def _():
        pl.semaphore_wait(barrier, count - 1)

    copies = {}
    for d in (4, 3, 5, 2, 6, 1, 7):
        to = (place + d) % count
        copies[d] = pltpu.make_async_remote_copy(
            src_ref=part_ref.at[to],
            dst_ref=held.at[place],
            send_sem=send_sem.at[d - 1],
            recv_sem=recv_sem.at[d - 1],
            device_id={"head": to},
            device_id_type=MESH,
        )
        copies[d].start()
    total = part_ref[place].astype(jnp.float32)
    for d in (1, 7, 2, 6, 3, 5, 4):
        copies[d].wait_recv()
        total = total + held[(place + count - d) % count].astype(jnp.float32)
    total_ref[...] = total.astype(total_ref.dtype)
    for copy in copies.values():
        copy.wait_send()

    @pl.when(away)
    def _():
        swap = pltpu.make_async_remote_copy(
            src_ref=total_ref,
            dst_ref=arrived,
            send_sem=swap_sem.at[0],
            recv_sem=swap_sem.at[1],
            device_id=mirror,
            device_id_type=MESH,
        )
        swap.start()
        swap.wait()
        mine = residual_ref[...].astype(jnp.float32) + arrived[...].astype(jnp.float32)
        out_ref[...] = mine.astype(out_ref.dtype)

    @pl.when(jnp.logical_not(away))
    def _():
        mine = residual_ref[...].astype(jnp.float32) + total_ref[...].astype(jnp.float32)
        out_ref[...] = mine.astype(out_ref.dtype)


def head_sum(parts, residual):
    block = pltpu.VMEM(residual.shape, residual.dtype)
    return pl.pallas_call(
        head_sum_kernel,
        name="head_sum",
        out_shape=jax.ShapeDtypeStruct(residual.shape, residual.dtype),
        in_specs=[pl.BlockSpec(memory_space=pltpu.VMEM)] * 2,
        out_specs=pl.BlockSpec(memory_space=pltpu.VMEM),
        scratch_shapes=[
            pltpu.VMEM(parts.shape, parts.dtype),
            block,
            block,
            pltpu.SemaphoreType.DMA((7,)),
            pltpu.SemaphoreType.DMA((7,)),
            pltpu.SemaphoreType.DMA((2,)),
        ],
        cost_estimate=pl.CostEstimate(flops=0, bytes_accessed=100_000_000, transcendentals=0),
        compiler_params=pltpu.CompilerParams(collective_id=2, has_side_effects=True),
    )(parts, residual)


def attention_kernel(q_ref, seg_ref, kv_ref, out_ref, qt_ref, top_ref, sum_ref, acc_ref):
    seq_place = lax.axis_index("seq")
    tokens = q_ref.shape[0]
    groups = q_ref.shape[1] // HEAD_SIZE
    span = KEY_BLOCKS * tokens
    factor = HEAD_SIZE ** (-0.5) * 1.4426950408889634
    table = jnp.sum(kv_ref[:, 2 * tokens :, :].astype(jnp.float32), axis=0)
    ids = lax.broadcasted_iota(jnp.int32, table.shape, 0)
    first = jnp.sum(jnp.where(ids == seg_ref[...], table, 0.0), axis=0, keepdims=True)
    lowest = jnp.min(first).astype(jnp.int32)
    highest = jnp.max(first).astype(jnp.int32)
    start = jnp.concatenate([first.astype(jnp.int32)] * groups, axis=1)
    place = lax.broadcasted_iota(jnp.int32, (1, tokens), 1) + seq_place * tokens
    place = jnp.concatenate([place] * groups, axis=1)
    for g in range(groups):
        qt_ref[g * tokens : (g + 1) * tokens, :] = q_ref[:, g * HEAD_SIZE : (g + 1) * HEAD_SIZE]
    top_ref[...] = jnp.full(top_ref.shape, -1e29, jnp.float32)
    sum_ref[...] = jnp.zeros(sum_ref.shape, jnp.float32)
    acc_ref[...] = jnp.zeros(acc_ref.shape, jnp.float32)

    def step(masked, i, carry):
        blocks = pl.ds(i * KEY_BLOCKS, KEY_BLOCKS)
        keys = kv_ref[blocks, 0:tokens, :].reshape(span, HEAD_SIZE)
        values = kv_ref[blocks, tokens : 2 * tokens, :].reshape(span, HEAD_SIZE)
        scores = lax.dot_general(
            keys, qt_ref[...], (((1,), (1,)), ((), ())), preferred_element_type=jnp.float32
        )
        if masked:
            key_place = lax.broadcasted_iota(jnp.int32, scores.shape, 0) + i * span
            allowed = (key_place >= start) & (key_place <= place)
            scores = jnp.where(allowed, scores, -1e30)
        old = top_ref[...]
        top = jnp.maximum(old, jnp.max(scores, axis=0, keepdims=True))
        weights = jnp.exp2((scores - top) * factor)
        shrink = jnp.exp2((old - top) * factor)
        top_ref[...] = top
        sum_ref[...] = sum_ref[...] * shrink + jnp.sum(weights, axis=0, keepdims=True)
        acc_ref[...] = acc_ref[...] * shrink + lax.dot_general(
            values,
            weights.astype(jnp.bfloat16),
            (((0,), (0,)), ((), ())),
            preferred_element_type=jnp.float32,
        )
        return carry

    begin = lowest // span
    end = (seq_place * tokens + tokens - 1) // span + 1
    clear_begin = jnp.minimum((highest + span - 1) // span, end)
    clear_end = jnp.maximum((seq_place * tokens + 1) // span, clear_begin)
    lax.fori_loop(begin, clear_begin, functools.partial(step, True), 0)
    lax.fori_loop(clear_begin, clear_end, functools.partial(step, False), 0)
    lax.fori_loop(clear_end, end, functools.partial(step, True), 0)
    result = acc_ref[...] / sum_ref[...]
    for g in range(groups):
        columns = slice(g * tokens, (g + 1) * tokens)
        out_ref[:, g * HEAD_SIZE : (g + 1) * HEAD_SIZE] = result[:, columns].T.astype(out_ref.dtype)


def attend(queries, segments, kv_all):
    tokens, width = queries.shape
    count = tokens * (width // HEAD_SIZE)
    return pl.pallas_call(
        attention_kernel,
        name="attend",
        out_shape=jax.ShapeDtypeStruct(queries.shape, queries.dtype),
        in_specs=[pl.BlockSpec(memory_space=pltpu.VMEM)] * 3,
        out_specs=pl.BlockSpec(memory_space=pltpu.VMEM),
        scratch_shapes=[
            pltpu.VMEM((count, HEAD_SIZE), jnp.bfloat16),
            pltpu.VMEM((1, count), jnp.float32),
            pltpu.VMEM((1, count), jnp.float32),
            pltpu.VMEM((HEAD_SIZE, count), jnp.float32),
        ],
        cost_estimate=pl.CostEstimate(flops=0, bytes_accessed=100_000_000, transcendentals=0),
    )(queries, segments, kv_all)


def on_device(
    block_query_rows,
    block_key_rows,
    block_value_rows,
    stretch_segments,
    residual,
    out_weight,
    cache_by_prefill,
    request_pages,
    request_owner,
):
    seq_count = lax.axis_size("seq")
    seq_place = lax.axis_index("seq")
    ids = jnp.arange(REQUESTS, dtype=jnp.int32)
    before = jnp.sum((stretch_segments[None, :] < ids[:, None]).astype(jnp.float32), axis=1)
    table = jnp.broadcast_to(before[:, None], (REQUESTS, HEAD_SIZE)).astype(jnp.bfloat16)
    kv_block = jnp.concatenate([block_key_rows, block_value_rows, table], axis=0)
    kv_all, w_all = gather_blocks(kv_block, out_weight.T, seq_count)
    local_pages = cache_by_prefill.shape[2]
    capacity = 2 * local_pages
    per_pair = capacity // seq_count
    owners = jnp.arange(seq_count, dtype=jnp.int32)
    run_pages = jnp.sum(
        jnp.where(request_owner[None, :] == owners[:, None], request_pages[None, :], 0), axis=1
    )
    run_start = jnp.sum(
        jnp.where(request_owner[None, :] < owners[:, None], request_pages[None, :], 0), axis=1
    )
    pair_slots = jnp.arange(per_pair, dtype=jnp.int32)
    offset = (seq_place - run_start) % seq_count
    slot_index = pair_slots[None, :] * seq_count + offset[:, None]
    sending = slot_index < run_pages[:, None]
    local_index = pair_slots[None, :] + ((run_start + offset - seq_place) // seq_count)[:, None]
    local_index = jnp.where(sending, local_index, 0).reshape(-1)
    picked = jnp.take(cache_by_prefill, local_index, axis=2)
    outgoing = jnp.where(
        sending.reshape(-1)[None, None, :, None, None], picked, jnp.zeros_like(picked)
    )
    outgoing, kv_all = lax.optimization_barrier((outgoing, kv_all))
    incoming = lax.all_to_all(outgoing, "seq", split_axis=2, concat_axis=2, tiled=True)
    attention = attend(block_query_rows, stretch_segments[None, :], kv_all)
    attention_all = ring_gather(attention)
    attention_all, incoming = lax.optimization_barrier((attention_all, incoming))
    rows, width = attention.shape
    partial_sums = lax.dot_general(
        attention_all.reshape(Z * rows, width),
        w_all.reshape(width, width),
        (((1,), (1,)), ((), ())),
        preferred_element_type=jnp.float32,
    ).astype(jnp.bfloat16)
    layer_out = head_sum(partial_sums.reshape(Z, rows, width), residual)
    layers, pair_kv, _, page_len, width = incoming.shape
    arranged = jnp.swapaxes(
        incoming.reshape(layers, pair_kv, seq_count, per_pair, page_len, width), 2, 3
    )
    my_start = run_start[seq_place]
    my_pages = run_pages[seq_place]
    rotated = jnp.roll(arranged, -my_start, axis=3).reshape(
        layers, pair_kv, capacity, page_len, width
    )
    keep = jnp.arange(capacity, dtype=jnp.int32) < my_pages
    cache_decode = jnp.where(keep[None, None, :, None, None], rotated, jnp.zeros_like(rotated))
    return (layer_out, cache_decode)


def solution(mesh):
    return jax.shard_map(
        on_device,
        mesh=mesh,
        in_specs=(
            P("seq", "head"),
            P("seq", "head"),
            P("seq", "head"),
            P("seq"),
            P("seq", "head"),
            P("head", "seq"),
            P(None, None, "seq", None, "head"),
            P(),
            P(),
        ),
        out_specs=(P("seq", "head"), P(None, None, "seq", None, "head")),
        check_vma=False,
    )
```

```python
import functools

import jax
import jax.numpy as jnp
from jax import lax
from jax.experimental import pallas as pl
from jax.experimental.pallas import tpu as pltpu
from jax.sharding import PartitionSpec as P

HEAD_SIZE = 128
Z = 8
Y = 4
REQUESTS = 16
MESH = pl.DeviceIdType.MESH
KEY_BLOCKS = 8


def seq_id(z, y, c):
    return z * 8 + y * 2 + c


def meet(partners):
    barrier = pltpu.get_barrier_semaphore()
    for seq in partners:
        pl.semaphore_signal(barrier, inc=1, device_id={"seq": seq}, device_id_type=MESH)
    pl.semaphore_wait(barrier, len(partners))


def gather_kernel(kv_ref, w_ref, kv_all, w_all, send_sem, recv_sem, local_sem):
    me = lax.axis_index("seq")
    z, y, c = me // 8, (me // 2) % 4, me % 2
    rows = kv_ref.shape[0]
    cut = 144
    across = seq_id(z, y, 1 - c)
    up, down = seq_id((z + 1) % Z, y, c), seq_id((z + 7) % Z, y, c)
    meet([across, up, down] + [seq_id(z, (y + a) % Y, c) for a in (1, 3)])

    used = [0]
    pending = []

    def send(src, dst, device):
        i = used[0]
        used[0] += 1
        copy = pltpu.make_async_remote_copy(
            src_ref=src,
            dst_ref=dst,
            send_sem=send_sem.at[i],
            recv_sem=recv_sem.at[i],
            device_id={"seq": device},
            device_id_type=MESH,
        )
        copy.start()
        pending.append(copy)
        return copy

    def kv_at(seq, part):
        lo, hi = part
        return kv_all.at[seq, pl.ds(lo, hi - lo)]

    whole = (0, rows)
    to_core = []
    own_kv = kv_all.at[me]
    ring = {}
    ring[0, 1, 1] = send(kv_ref, own_kv, up)
    ring[0, -1, 1] = send(kv_ref, own_kv, down)
    near = {}
    left, right = seq_id(z, (y + 3) % Y, c), seq_id(z, (y + 1) % Y, c)
    near[1] = [send(kv_ref, own_kv, left)]
    near[3] = [send(kv_ref, own_kv, right)]
    near[2] = []
    to_core.append(send(kv_ref, own_kv, across))
    w_slot = y * 2 + c
    local = [
        pltpu.make_async_copy(kv_ref, own_kv, local_sem.at[0]),
        pltpu.make_async_copy(w_ref, w_all.at[w_slot], local_sem.at[1]),
    ]
    for copy in local:
        copy.start()

    def start_chain(a):
        seq = seq_id(z, (y + a) % Y, c)
        for copy in near[a]:
            copy.wait_recv()
        block = kv_at(seq, whole)
        if a == 1:
            half = kv_at(seq, (0, cut))
            near[2].append(send(half, half, left))
        if a == 3:
            half = kv_at(seq, (cut, rows))
            near[2].append(send(half, half, right))
        ring[a, 1, 1] = send(block, block, up)
        ring[a, -1, 1] = send(block, block, down)
        to_core.append(send(block, block, across))

    def advance(a, k):
        for direction, target in ((1, up), (-1, down)):
            seq = seq_id((z + 8 - direction * k) % Z, (y + a) % Y, c)
            ring[a, direction, k].wait_recv()
            part = whole
            if k == 4:
                part = (0, cut) if direction == 1 else (cut, rows)
            block = kv_at(seq, part)
            if k < 4:
                onward = block
                if k == 3:
                    onward = kv_at(seq, (0, cut) if direction == 1 else (cut, rows))
                ring[a, direction, k + 1] = send(onward, onward, target)
            to_core.append(send(block, block, across))

    near_w = {2: []}

    def send_weight():
        mine = w_all.at[w_slot]
        near_w[1] = [send(w_ref, mine, left)]
        near_w[3] = [send(w_ref, mine, right)]
        to_core.append(send(w_ref, mine, across))

    def weight_from(a):
        slot = (y + a) % Y * 2 + c
        block = w_all.at[slot]
        for copy in near_w[a]:
            copy.wait_recv()
        if a == 1:
            half = block.at[pl.ds(0, 48)]
            near_w[2].append(send(half, half, left))
        if a == 3:
            half = block.at[pl.ds(48, 32)]
            near_w[2].append(send(half, half, right))
        to_core.append(send(block, block, across))

    delay = {0: 0, 1: 1, 3: 1, 2: 3}
    for tick in range(1, 8):
        for a, late in delay.items():
            k = tick - late
            if k == 0:
                start_chain(a)
            elif 1 <= k <= 4:
                advance(a, k)
        if tick == 1:
            send_weight()
        if tick == 4:
            weight_from(1)
            weight_from(3)
    weight_from(2)
    for copy in to_core:
        copy.wait_recv()
    for copy in pending:
        copy.wait_send()
    for copy in local:
        copy.wait()


def gather_blocks(kv_block, w_block, seq_count):
    sems = 84
    return pl.pallas_call(
        gather_kernel,
        name="gather_blocks",
        out_shape=(
            jax.ShapeDtypeStruct((seq_count,) + kv_block.shape, kv_block.dtype),
            jax.ShapeDtypeStruct((2 * Y,) + w_block.shape, w_block.dtype),
        ),
        in_specs=[pl.BlockSpec(memory_space=pltpu.VMEM)] * 2,
        out_specs=[pl.BlockSpec(memory_space=pl.ANY)] * 2,
        scratch_shapes=[
            pltpu.SemaphoreType.DMA((sems,)),
            pltpu.SemaphoreType.DMA((sems,)),
            pltpu.SemaphoreType.DMA((2,)),
        ],
        compiler_params=pltpu.CompilerParams(collective_id=0, has_side_effects=True),
    )(kv_block, w_block)


def ring_kernel(x_ref, all_ref, send_sem, recv_sem, local_sem):
    me = lax.axis_index("seq")
    z, y, c = me // 8, (me // 2) % 4, me % 2
    rows = x_ref.shape[0]
    half = rows // 2
    up, down = seq_id((z + 1) % Z, y, c), seq_id((z + 7) % Z, y, c)
    meet([up, down])
    pending = []
    ring = {}

    def send(src, dst, device, direction, k):
        i = 2 * (k - 1) + (direction > 0)
        copy = pltpu.make_async_remote_copy(
            src_ref=src,
            dst_ref=dst,
            send_sem=send_sem.at[i],
            recv_sem=recv_sem.at[i],
            device_id={"seq": device},
            device_id_type=MESH,
        )
        copy.start()
        pending.append(copy)
        ring[direction, k] = copy

    send(x_ref, all_ref.at[z], up, 1, 1)
    send(x_ref, all_ref.at[z], down, -1, 1)
    local = pltpu.make_async_copy(x_ref, all_ref.at[z], local_sem)
    local.start()
    for k in (1, 2, 3, 4):
        for direction, target in ((1, up), (-1, down)):
            ring[direction, k].wait_recv()
            if k < 4:
                block = all_ref.at[(z + 8 - direction * k) % Z]
                if k == 3:
                    block = block.at[pl.ds(0, half)] if direction == 1 else block.at[pl.ds(half, half)]
                send(block, block, target, direction, k + 1)
    for copy in pending:
        copy.wait_send()
    local.wait()


def ring_gather(x):
    return pl.pallas_call(
        ring_kernel,
        name="ring_gather",
        out_shape=jax.ShapeDtypeStruct((Z,) + x.shape, x.dtype),
        in_specs=[pl.BlockSpec(memory_space=pltpu.VMEM)],
        out_specs=pl.BlockSpec(memory_space=pl.ANY),
        scratch_shapes=[
            pltpu.SemaphoreType.DMA((8,)),
            pltpu.SemaphoreType.DMA((8,)),
            pltpu.SemaphoreType.DMA,
        ],
        compiler_params=pltpu.CompilerParams(collective_id=1, has_side_effects=True),
    )(x)


def attention_kernel(q_ref, seg_ref, kv_ref, out_ref, qt_ref, top_ref, sum_ref, acc_ref):
    seq_place = lax.axis_index("seq")
    tokens = q_ref.shape[0]
    groups = q_ref.shape[1] // HEAD_SIZE
    span = KEY_BLOCKS * tokens
    factor = HEAD_SIZE ** (-0.5) * 1.4426950408889634
    table = jnp.sum(kv_ref[:, 2 * tokens :, :].astype(jnp.float32), axis=0)
    ids = lax.broadcasted_iota(jnp.int32, table.shape, 0)
    first = jnp.sum(jnp.where(ids == seg_ref[...], table, 0.0), axis=0, keepdims=True)
    lowest = jnp.min(first).astype(jnp.int32)
    highest = jnp.max(first).astype(jnp.int32)
    start = jnp.concatenate([first.astype(jnp.int32)] * groups, axis=1)
    place = lax.broadcasted_iota(jnp.int32, (1, tokens), 1) + seq_place * tokens
    place = jnp.concatenate([place] * groups, axis=1)
    for g in range(groups):
        qt_ref[g * tokens : (g + 1) * tokens, :] = q_ref[:, g * HEAD_SIZE : (g + 1) * HEAD_SIZE]
    top_ref[...] = jnp.full(top_ref.shape, -1e29, jnp.float32)
    sum_ref[...] = jnp.zeros(sum_ref.shape, jnp.float32)
    acc_ref[...] = jnp.zeros(acc_ref.shape, jnp.float32)

    def step(masked, i, carry):
        blocks = pl.ds(i * KEY_BLOCKS, KEY_BLOCKS)
        keys = kv_ref[blocks, 0:tokens, :].reshape(span, HEAD_SIZE)
        values = kv_ref[blocks, tokens : 2 * tokens, :].reshape(span, HEAD_SIZE)
        scores = lax.dot_general(
            keys, qt_ref[...], (((1,), (1,)), ((), ())), preferred_element_type=jnp.float32
        )
        if masked:
            key_place = lax.broadcasted_iota(jnp.int32, scores.shape, 0) + i * span
            allowed = (key_place >= start) & (key_place <= place)
            scores = jnp.where(allowed, scores, -1e30)
        old = top_ref[...]
        top = jnp.maximum(old, jnp.max(scores, axis=0, keepdims=True))
        weights = jnp.exp2((scores - top) * factor)
        shrink = jnp.exp2((old - top) * factor)
        top_ref[...] = top
        sum_ref[...] = sum_ref[...] * shrink + jnp.sum(weights, axis=0, keepdims=True)
        acc_ref[...] = acc_ref[...] * shrink + lax.dot_general(
            values,
            weights.astype(jnp.bfloat16),
            (((0,), (0,)), ((), ())),
            preferred_element_type=jnp.float32,
        )
        return carry

    begin = lowest // span
    end = (seq_place * tokens + tokens - 1) // span + 1
    clear_begin = jnp.minimum((highest + span - 1) // span, end)
    clear_end = jnp.maximum((seq_place * tokens + 1) // span, clear_begin)
    lax.fori_loop(begin, clear_begin, functools.partial(step, True), 0)
    lax.fori_loop(clear_begin, clear_end, functools.partial(step, False), 0)
    lax.fori_loop(clear_end, end, functools.partial(step, True), 0)
    result = acc_ref[...] / sum_ref[...]
    for g in range(groups):
        columns = slice(g * tokens, (g + 1) * tokens)
        out_ref[:, g * HEAD_SIZE : (g + 1) * HEAD_SIZE] = result[:, columns].T.astype(out_ref.dtype)


def attend(queries, segments, kv_all):
    tokens, width = queries.shape
    count = tokens * (width // HEAD_SIZE)
    return pl.pallas_call(
        attention_kernel,
        name="attend",
        out_shape=jax.ShapeDtypeStruct(queries.shape, queries.dtype),
        in_specs=[pl.BlockSpec(memory_space=pltpu.VMEM)] * 3,
        out_specs=pl.BlockSpec(memory_space=pltpu.VMEM),
        scratch_shapes=[
            pltpu.VMEM((count, HEAD_SIZE), jnp.bfloat16),
            pltpu.VMEM((1, count), jnp.float32),
            pltpu.VMEM((1, count), jnp.float32),
            pltpu.VMEM((HEAD_SIZE, count), jnp.float32),
        ],
        cost_estimate=pl.CostEstimate(flops=0, bytes_accessed=100_000_000, transcendentals=0),
    )(queries, segments, kv_all)


def on_device(
    block_query_rows,
    block_key_rows,
    block_value_rows,
    stretch_segments,
    residual,
    out_weight,
    cache_by_prefill,
    request_pages,
    request_owner,
):
    seq_count = lax.axis_size("seq")
    head_count = lax.axis_size("head")
    seq_place = lax.axis_index("seq")
    ids = jnp.arange(REQUESTS, dtype=jnp.int32)
    before = jnp.sum((stretch_segments[None, :] < ids[:, None]).astype(jnp.float32), axis=1)
    table = jnp.broadcast_to(before[:, None], (REQUESTS, HEAD_SIZE)).astype(jnp.bfloat16)
    kv_block = jnp.concatenate([block_key_rows, block_value_rows, table], axis=0)
    kv_all, w_all = gather_blocks(kv_block, out_weight.T, seq_count)
    local_pages = cache_by_prefill.shape[2]
    capacity = 2 * local_pages
    per_pair = capacity // seq_count
    owners = jnp.arange(seq_count, dtype=jnp.int32)
    run_pages = jnp.sum(
        jnp.where(request_owner[None, :] == owners[:, None], request_pages[None, :], 0), axis=1
    )
    run_start = jnp.sum(
        jnp.where(request_owner[None, :] < owners[:, None], request_pages[None, :], 0), axis=1
    )
    pair_slots = jnp.arange(per_pair, dtype=jnp.int32)
    offset = (seq_place - run_start) % seq_count
    slot_index = pair_slots[None, :] * seq_count + offset[:, None]
    sending = slot_index < run_pages[:, None]
    local_index = pair_slots[None, :] + ((run_start + offset - seq_place) // seq_count)[:, None]
    local_index = jnp.where(sending, local_index, 0).reshape(-1)
    picked = jnp.take(cache_by_prefill, local_index, axis=2)
    outgoing = jnp.where(
        sending.reshape(-1)[None, None, :, None, None], picked, jnp.zeros_like(picked)
    )
    outgoing, kv_all = lax.optimization_barrier((outgoing, kv_all))
    early = lax.all_to_all(outgoing[:1], "seq", split_axis=2, concat_axis=2, tiled=True)
    attention = attend(block_query_rows, stretch_segments[None, :], kv_all)
    attention_all = ring_gather(attention)
    attention_all, early = lax.optimization_barrier((attention_all, early))
    rows, width = attention.shape
    partial_sums = lax.dot_general(
        attention_all.reshape(Z * rows, width),
        w_all.reshape(width, width),
        (((1,), (1,)), ((), ())),
        preferred_element_type=jnp.float32,
    ).astype(jnp.bfloat16)
    parts = lax.all_to_all(
        partial_sums.reshape(Z, rows, width), "head", split_axis=0, concat_axis=0, tiled=True
    )
    parts, outgoing = lax.optimization_barrier((parts, outgoing))
    late = lax.all_to_all(outgoing[1:], "seq", split_axis=2, concat_axis=2, tiled=True)
    incoming = jnp.concatenate([early, late], axis=0)
    total = jnp.sum(parts.astype(jnp.float32), axis=0).astype(jnp.bfloat16)
    pairs = [
        ((z * 8 + rest) * head_count + h, (h * 8 + rest) * head_count + z)
        for z in range(Z)
        for rest in range(8)
        for h in range(head_count)
    ]
    mine = lax.ppermute(total, ("seq", "head"), pairs)
    layer_out = (residual.astype(jnp.float32) + mine.astype(jnp.float32)).astype(jnp.bfloat16)
    layers, pair_kv, _, page_len, width = incoming.shape
    arranged = jnp.swapaxes(
        incoming.reshape(layers, pair_kv, seq_count, per_pair, page_len, width), 2, 3
    )
    my_start = run_start[seq_place]
    my_pages = run_pages[seq_place]
    rotated = jnp.roll(arranged, -my_start, axis=3).reshape(
        layers, pair_kv, capacity, page_len, width
    )
    keep = jnp.arange(capacity, dtype=jnp.int32) < my_pages
    cache_decode = jnp.where(keep[None, None, :, None, None], rotated, jnp.zeros_like(rotated))
    return (layer_out, cache_decode)


def solution(mesh):
    return jax.shard_map(
        on_device,
        mesh=mesh,
        in_specs=(
            P("seq", "head"),
            P("seq", "head"),
            P("seq", "head"),
            P("seq"),
            P("seq", "head"),
            P("head", "seq"),
            P(None, None, "seq", None, "head"),
            P(),
            P(),
        ),
        out_specs=(P("seq", "head"), P(None, None, "seq", None, "head")),
        check_vma=False,
    )
```
